32 devices in a mesh: shard: 4 (over y, core), rep: 8 (over z, x).
Axes of the slice: x: 2, y: 2, z: 4, core: 2. Of those that a mesh axis runs over, the one named last changes fastest.
Arguments:
- tokens: bfloat16 [8, 512, 768], P('rep', 'shard'), may hold values from -6 to 6
- gain_one: bfloat16 [768], P('shard'), may hold values from 0.5 to 1.5
- qkv_weight: bfloat16 [768, 2304], P('shard'), may hold values from -6 to 6
- out_weight: bfloat16 [768, 768], P('shard'), may hold values from -2.5 to 2.5
- gain_two: bfloat16 [768], P('shard'), may hold values from 0.5 to 1.5
- in_weight: bfloat16 [768, 2304], P('shard'), may hold values from -0.21875 to 0.21875
- down_weight: bfloat16 [1152, 768], P('shard'), may hold values from -0.1875 to 0.1875
- grad_output: bfloat16 [8, 512, 768], P('rep', 'shard'), may hold values from -6 to 6
Outputs:
- output: bfloat16 [8, 512, 768], P('rep', 'shard')
- grad_tokens: float32 [8, 512, 768], P('rep', 'shard')
- grad_gain_one: float32 [768], P('shard')
- grad_qkv: float32 [768, 2304], P('shard')
- grad_out: float32 [768, 768], P('shard')
- grad_gain_two: float32 [768], P('shard')
- grad_in: float32 [768, 2304], P('shard')
- grad_down: float32 [1152, 768], P('shard')
The draws below stay inside these ranges and needn't reach their ends.
All inputs are finite; a program needn't handle non-finite values.
Results may differ from the reference program's by a relative error of at most 0.02.
Values may be sent and summed in bfloat16 or wider, within the bound.
A program may use at most 128 MiB of HBM per device.

```python
import jax
import jax.numpy as jnp
from jax import lax

D = 768
HEADS = 12
HEAD_DIM = 64
FF = 1152
TOK_DEV = 128
LEN = 512
SEQS = 8
N_SHARD = 4


def draw_qkv_weight(key, part):
    base = jnp.clip(jax.random.normal(key, (D, 3 * D), jnp.float32), -5.0, 5.0) * D ** (-0.5)
    return base.astype(jnp.bfloat16)


def block_levels(stream_key, dims, pieces, smallest, largest):
    level, own = 1.0, jax.random.fold_in(stream_key, 6)
    for dim, shards_of in pieces:
        heights = jnp.exp(jax.random.uniform(jax.random.fold_in(own, dim), (shards_of,), jnp.float32, smallest / len(pieces), largest / len(pieces)))
        level = level * jnp.repeat(heights, dims[dim] // shards_of).reshape([-1 if axis == dim else 1 for axis in range(len(dims))])
    return level


def scatter_about(rng, shape, deviation, bound, cuts=(), held_as=jnp.bfloat16):
    loudness = block_levels(rng, shape, cuts, -0.22, 0.18) if cuts else 1.0
    values = jax.random.normal(rng, shape, jnp.float32) * deviation * loudness
    return jnp.minimum(jnp.maximum(values, -bound), bound).astype(held_as)


def setup_inputs(seed: int = 0) -> dict:
    streams_of = jax.random.split(jax.random.key(seed), 9)
    return {
        "tokens": scatter_about(streams_of[0], (SEQS, LEN, D), 1.0, 6.0, ((0, 8), (1, 4))),
        "gain_one": jnp.clip(1.0 + 0.1 * jax.random.normal(streams_of[1], (D,), jnp.float32), 0.5, 1.5).astype(jnp.bfloat16),
        "qkv_weight": draw_qkv_weight(jax.random.fold_in(streams_of[8], 71), 0),
        "out_weight": scatter_about(streams_of[3], (D, D), (max(1, 4 * D // (TOK_DEV * N_SHARD))) ** -0.5, 2.5, ((0, 4),)),
        "gain_two": jnp.clip(1.0 + 0.1 * jax.random.normal(streams_of[4], (D,), jnp.float32), 0.5, 1.5).astype(jnp.bfloat16),
        "in_weight": scatter_about(streams_of[5], (D, 2 * FF), D ** -0.5, 0.21875, ((0, 4),)),
        "down_weight": scatter_about(streams_of[6], (FF, D), FF ** -0.5, 0.1875, ((0, 4),)),
        "grad_output": scatter_about(streams_of[7], (SEQS, LEN, D), 1.0, 6.0, ((0, 8), (1, 4))),
    }


EPSILON = 1e-05
THETA = 160000.0
SQRT_HALF = 0.7071067811865476
INV_SQRT_TAU = 0.3989422804014327

def layer_norm(values, gain):
    mean_row = lax.optimization_barrier(jnp.mean(values, axis=-1, keepdims=True))
    centred = values - mean_row
    variance = lax.optimization_barrier(jnp.mean(centred * centred, axis=-1, keepdims=True))
    inverse = lax.rsqrt(variance + EPSILON)
    normed = centred * inverse
    return (normed, inverse, normed * gain.astype(jnp.float32))

def norm_backward(grad_out, normed, inverse, gain):
    grad_normed = grad_out * gain.astype(jnp.float32)
    gain_grad = lax.optimization_barrier(jnp.sum(grad_out * normed, axis=0))
    first = lax.optimization_barrier(jnp.mean(grad_normed, axis=-1, keepdims=True))
    second = lax.optimization_barrier(jnp.mean(grad_normed * normed, axis=-1, keepdims=True))
    return (inverse * (grad_normed - first - normed * second), gain_grad)

def rotary_tables(positions, head_dim):
    half = head_dim // 2
    freq = THETA ** (-jnp.arange(half, dtype=jnp.float32) * 2.0 / head_dim)
    angles = positions.astype(jnp.float32)[:, None] * freq[None, :]
    angles = jnp.concatenate([angles, angles], axis=-1)
    return (jnp.cos(angles)[:, None, :], jnp.sin(angles)[:, None, :])

def rotate_half(values):
    half = values.shape[-1] // 2
    return jnp.concatenate([-values[..., half:], values[..., :half]], axis=-1)

def gelu_pair(inner):
    cdf = 0.5 * (1.0 + jax.scipy.special.erf(inner * SQRT_HALF))
    return (inner * cdf, cdf + inner * jnp.exp(-0.5 * inner * inner) * INV_SQRT_TAU)

def as_operand(values):
    return lax.optimization_barrier(values.astype(jnp.bfloat16)).astype(jnp.float32)

def sequence_pass(x_seq, grad_seq, gain_one, qkv_weight, out_weight, gain_two, in_weight, down_weight):
    length = x_seq.shape[0]
    scale = HEAD_DIM ** (-0.5)
    inputs = x_seq.astype(jnp.float32)
    normed_one, inverse_one, scaled_one = layer_norm(inputs, gain_one)
    hidden_one = scaled_one.astype(jnp.bfloat16)
    projected = jnp.dot(hidden_one, qkv_weight, preferred_element_type=jnp.float32)
    cosine, sine = rotary_tables(jnp.arange(length, dtype=jnp.int32), HEAD_DIM)
    queries = projected[:, :D].reshape(length, HEADS, HEAD_DIM)
    key_raw = projected[:, D:2 * D].reshape(length, HEADS, HEAD_DIM)
    query_rot = as_operand(queries * cosine + rotate_half(queries) * sine)
    key_rot = as_operand(key_raw * cosine + rotate_half(key_raw) * sine)
    value_rot = as_operand(projected[:, 2 * D:].reshape(length, HEADS, HEAD_DIM))
    scores = jnp.einsum('qhd,khd->hqk', query_rot, key_rot) * scale
    maxima = lax.optimization_barrier(jnp.max(scores, axis=-1))
    expo = jnp.exp(scores - maxima[..., None])
    totals = lax.optimization_barrier(jnp.sum(expo, axis=-1))
    accum = jnp.einsum('hqk,khd->hqd', as_operand(expo), value_rot)
    attended = (accum / totals[..., None]).transpose(1, 0, 2).reshape(length, D).astype(jnp.bfloat16)
    log_sum = maxima + jnp.log(totals)
    resid = inputs + jnp.dot(attended, out_weight, preferred_element_type=jnp.float32)
    normed_two, inverse_two, scaled_two = layer_norm(resid, gain_two)
    hidden_two = scaled_two.astype(jnp.bfloat16)
    upper = jnp.dot(hidden_two, in_weight, preferred_element_type=jnp.float32)
    inner = upper[:, :FF]
    gate_half = upper[:, FF:]
    gelu_value, gelu_slope = gelu_pair(inner)
    act = (gelu_value * gate_half).astype(jnp.bfloat16)
    output = (resid + jnp.dot(act, down_weight, preferred_element_type=jnp.float32)).astype(jnp.bfloat16)
    grad_b = grad_seq
    grad_f = grad_seq.astype(jnp.float32)
    grad_down = jnp.dot(act.T, grad_b, preferred_element_type=jnp.float32)
    grad_act = jnp.dot(grad_b, down_weight.T, preferred_element_type=jnp.float32)
    grad_upper = jnp.concatenate([grad_act * gate_half * gelu_slope, grad_act * gelu_value], axis=-1).astype(jnp.bfloat16)
    grad_in = jnp.dot(hidden_two.T, grad_upper, preferred_element_type=jnp.float32)
    grad_h2 = jnp.dot(grad_upper, in_weight.T, preferred_element_type=jnp.float32)
    norm_grad_two, grad_gain_two = norm_backward(grad_h2, normed_two, inverse_two, gain_two)
    grad_resid = grad_f + norm_grad_two
    resid_b = grad_resid.astype(jnp.bfloat16)
    grad_out = jnp.dot(attended.T, resid_b, preferred_element_type=jnp.float32)
    grad_att = jnp.dot(resid_b, out_weight.T, preferred_element_type=jnp.float32).astype(jnp.bfloat16)
    grad_heads = grad_att.astype(jnp.float32).reshape(length, HEADS, HEAD_DIM)
    att_heads = attended.astype(jnp.float32).reshape(length, HEADS, HEAD_DIM)
    delta = lax.optimization_barrier(jnp.sum(grad_heads * att_heads, axis=-1)).T
    probs = jnp.exp(scores - log_sum[..., None])
    grad_value = jnp.einsum('hqk,qhd->khd', as_operand(probs), grad_heads)
    grad_probs = jnp.einsum('qhd,khd->hqk', grad_heads, value_rot)
    grad_scores = as_operand(probs * (grad_probs - delta[..., None]) * scale)
    grad_qr = jnp.einsum('hqk,khd->qhd', grad_scores, key_rot)
    grad_kr = jnp.einsum('hqk,qhd->khd', grad_scores, query_rot)
    grad_q = grad_qr * cosine - rotate_half(grad_qr) * sine
    grad_k = grad_kr * cosine - rotate_half(grad_kr) * sine
    grad_projected = jnp.concatenate([grad_q.reshape(length, D), grad_k.reshape(length, D), grad_value.reshape(length, D)], axis=-1).astype(jnp.bfloat16)
    grad_qkv = jnp.dot(hidden_one.T, grad_projected, preferred_element_type=jnp.float32)
    grad_h1 = jnp.dot(grad_projected, qkv_weight.T, preferred_element_type=jnp.float32)
    norm_grad_one, grad_gain_one = norm_backward(grad_h1, normed_one, inverse_one, gain_one)
    grad_tokens = grad_resid + norm_grad_one
    return (output, grad_tokens, (grad_gain_one, grad_qkv, grad_out, grad_gain_two, grad_in, grad_down))

def reference(tokens, gain_one, qkv_weight, out_weight, gain_two, in_weight, down_weight, grad_output):

    def step(carry, pair):
        output, grad_tokens, grads = sequence_pass(pair[0], pair[1], gain_one, qkv_weight, out_weight, gain_two, in_weight, down_weight)
        carry = tuple((total + part for total, part in zip(carry, grads)))
        return (carry, (output, grad_tokens))
    start = (jnp.zeros((D,), jnp.float32), jnp.zeros((D, 3 * D), jnp.float32), jnp.zeros((D, D), jnp.float32), jnp.zeros((D,), jnp.float32), jnp.zeros((D, 2 * FF), jnp.float32), jnp.zeros((FF, D), jnp.float32))
    sums, stacked = lax.scan(step, start, (tokens, grad_output))
    return (stacked[0], stacked[1], sums[0], sums[1], sums[2], sums[3], sums[4], sums[5])
```

```python
import functools

import jax
import jax.numpy as jnp
from jax import lax
from jax.experimental import pallas as pl
from jax.experimental.pallas import tpu as pltpu
from jax.sharding import PartitionSpec as P

HEAD_DIM = 64
EPSILON = 1e-05
THETA = 160000.0
SQRT_HALF = 0.7071067811865476
INV_SQRT_TAU = 0.3989422804014327
MESH_ID = pl.DeviceIdType.MESH
LANES = 128
VMEM = pl.BlockSpec(memory_space=pltpu.VMEM)


def layer_norm(values, gain):
    mean_row = jnp.mean(values, axis=-1, keepdims=True)
    centred = values - mean_row
    variance = jnp.mean(centred * centred, axis=-1, keepdims=True)
    inverse = lax.rsqrt(variance + EPSILON)
    normed = centred * inverse
    return (normed, inverse, normed * gain.astype(jnp.float32))


def norm_backward(grad_out, normed, inverse, gain):
    grad_normed = grad_out * gain.astype(jnp.float32)
    gain_grad = jnp.sum(grad_out * normed, axis=0)
    first = jnp.mean(grad_normed, axis=-1, keepdims=True)
    second = jnp.mean(grad_normed * normed, axis=-1, keepdims=True)
    return (inverse * (grad_normed - first - normed * second), gain_grad)


def rotary_tables(count, head_dim):
    half = head_dim // 2
    positions = jnp.arange(count, dtype=jnp.int32)
    freq = THETA ** (-jnp.arange(half, dtype=jnp.float32) * 2.0 / head_dim)
    angles = positions.astype(jnp.float32)[:, None] * freq[None, :]
    angles = jnp.concatenate([angles, angles], axis=-1)
    return (jnp.cos(angles)[None], jnp.sin(angles)[None])


def rotate_half(values):
    half = values.shape[-1] // 2
    return jnp.concatenate([-values[..., half:], values[..., :half]], axis=-1)


def gelu_pair(inner):
    cdf = 0.5 * (1.0 + jax.scipy.special.erf(inner * SQRT_HALF))
    return (inner * cdf, cdf + inner * jnp.exp(-0.5 * inner * inner) * INV_SQRT_TAU)


def outer_sum(left, right):
    return lax.dot_general(
        left, right, (((0,), (0,)), ((), ())), preferred_element_type=jnp.float32
    )


def times_transposed(left, weight):
    return lax.dot_general(
        left, weight, (((1,), (1,)), ((), ())), preferred_element_type=jnp.float32
    )


def flip(index, bit):
    return index + bit * (1 - 2 * ((index // bit) % 2))


def remote(src, dst, send, recv, axis, target):
    return pltpu.make_async_remote_copy(
        src_ref=src,
        dst_ref=dst,
        send_sem=send,
        recv_sem=recv,
        device_id={axis: target},
        device_id_type=MESH_ID,
    )


def greet(partners):
    barrier = pltpu.get_barrier_semaphore()
    for axis, target in partners:
        pl.semaphore_signal(barrier, inc=1, device_id={axis: target}, device_id_type=MESH_ID)
    pl.semaphore_wait(barrier, len(partners))


def shard_partners(me):
    return [("shard", flip(me, 1)), ("shard", flip(me, 2)), ("shard", flip(flip(me, 1), 2))]


def gather_kernel(gathered, swapped, *refs):
    total = gathered + swapped
    ins, outs = refs[:total], refs[total : 2 * total]
    send, recv, local_sem = refs[2 * total :]
    me = lax.axis_index("shard")
    partners = shard_partners(me)
    greet(partners)
    (_, core), (_, chip), (_, diagonal) = partners
    pending = []
    sent = []
    for i in range(gathered):
        far = remote(ins[i], outs[i].at[me], send.at[i, 0], recv.at[i, 0], "shard", chip)
        far.start()
        near = remote(ins[i], outs[i].at[me], send.at[i, 1], recv.at[i, 1], "shard", core)
        near.start()
        own = pltpu.make_async_copy(ins[i], outs[i].at[me], local_sem.at[i])
        own.start()
        pending.append((far, near, own))
    for i in range(gathered, total):
        copies = []
        for k, target in enumerate((chip, diagonal, core)):
            copy = remote(
                ins[i].at[target], outs[i].at[me], send.at[i, k], recv.at[i, k], "shard", target
            )
            copy.start()
            copies.append(copy)
        own = pltpu.make_async_copy(ins[i].at[me], outs[i].at[me], local_sem.at[i])
        own.start()
        sent.append((copies, own))
    for i in range(gathered):
        pending[i][0].wait_recv()
        relay = remote(
            outs[i].at[chip], outs[i].at[chip], send.at[i, 2], recv.at[i, 2], "shard", core
        )
        relay.start()
        pending[i] = pending[i] + (relay,)
    for far, near, own, relay in pending:
        far.wait_send()
        near.wait()
        own.wait()
        relay.wait()
    for copies, own in sent:
        for copy in copies:
            copy.wait()
        own.wait()


def gather(collective, gathered, swapped, n_shard):
    arrays = tuple(gathered) + tuple(swapped)
    shapes = [jax.ShapeDtypeStruct((n_shard,) + a.shape, a.dtype) for a in gathered]
    shapes += [jax.ShapeDtypeStruct(a.shape, a.dtype) for a in swapped]
    return pl.pallas_call(
        functools.partial(gather_kernel, len(gathered), len(swapped)),
        out_shape=tuple(shapes),
        in_specs=[VMEM] * len(arrays),
        out_specs=tuple([VMEM] * len(arrays)),
        scratch_shapes=[
            pltpu.SemaphoreType.DMA((len(arrays), 3)),
            pltpu.SemaphoreType.DMA((len(arrays), 3)),
            pltpu.SemaphoreType.DMA((len(arrays),)),
        ],
        compiler_params=pltpu.CompilerParams(collective_id=collective, has_side_effects=True),
    )(*arrays)


def scatter_kernel(total, *refs):
    ins, outs = refs[:total], refs[total : 2 * total]
    near_buf, out_buf, far_buf, send, recv = refs[2 * total :]
    me = lax.axis_index("shard")
    partners = shard_partners(me)[:2]
    greet(partners)
    (_, core), (_, chip) = partners
    diagonal = flip(core, 2)
    first, second, third = [], [], []
    for i in range(total):
        a = remote(
            ins[i].at[diagonal], near_buf.at[i, 0], send.at[i, 0], recv.at[i, 0], "shard", core
        )
        a.start()
        b = remote(ins[i].at[core], near_buf.at[i, 1], send.at[i, 1], recv.at[i, 1], "shard", core)
        b.start()
        first.append(a)
        second.append(b)
    for i in range(total):
        first[i].wait_recv()
        out_buf[i] = (
            ins[i][chip].astype(jnp.float32) + near_buf[i, 0].astype(jnp.float32)
        ).astype(jnp.bfloat16)
        c = remote(out_buf.at[i], far_buf.at[i], send.at[i, 2], recv.at[i, 2], "shard", chip)
        c.start()
        third.append(c)
    for i in range(total):
        second[i].wait_recv()
        outs[i][...] = ins[i][me].astype(jnp.float32) + near_buf[i, 1].astype(jnp.float32)
    for i in range(total):
        third[i].wait_recv()
        outs[i][...] += far_buf[i].astype(jnp.float32)
    for i in range(total):
        first[i].wait_send()
        second[i].wait_send()
        third[i].wait_send()


def scatter(collective, arrays):
    total = len(arrays)
    block = arrays[0].shape[1:]
    return pl.pallas_call(
        functools.partial(scatter_kernel, total),
        out_shape=tuple([jax.ShapeDtypeStruct(block, jnp.float32)] * total),
        in_specs=[VMEM] * total,
        out_specs=tuple([VMEM] * total),
        scratch_shapes=[
            pltpu.VMEM((total, 2) + block, jnp.bfloat16),
            pltpu.VMEM((total,) + block, jnp.bfloat16),
            pltpu.VMEM((total,) + block, jnp.bfloat16),
            pltpu.SemaphoreType.DMA((total, 3)),
            pltpu.SemaphoreType.DMA((total, 3)),
        ],
        compiler_params=pltpu.CompilerParams(collective_id=collective, has_side_effects=True),
    )(*arrays)


def halves(order, me):
    length = 1 << len(order)
    offset = 0
    plan = []
    for bit in order:
        length //= 2
        side = (me // bit) % 2
        plan.append((bit, offset + side * length, offset + (1 - side) * length, length))
        offset = offset + side * length
    return plan


def sum_kernel(streams, *refs):
    total = len(streams)
    ins, outs = refs[:total], refs[total : 2 * total]
    acc, box = refs[2 * total : 3 * total], refs[3 * total : 4 * total]
    send, recv, swap_send, swap_recv, local_sem = refs[4 * total :]
    rep = lax.axis_index("rep")
    me = lax.axis_index("shard")
    bits = sorted(streams[0][0])
    steps = len(bits)
    group = shard_partners(me)
    greet([("rep", flip(rep, bit)) for bit in bits] + group)
    plans = [halves(order, rep) for order, _ in streams]
    started = [[] for _ in streams]

    def begin(i, k):
        order, swap = streams[i]
        plan = plans[i]
        if k < steps:
            bit, kept, sent, length = plan[k]
            source = ins[i] if k == 0 else acc[i]
            copy = remote(
                source.at[pl.ds(sent, length)],
                box[i].at[pl.ds(length, length)],
                send.at[i, k],
                recv.at[i, k],
                "rep",
                flip(rep, bit),
            )
            copy.start()
            started[i].append([copy])
        elif k == steps:
            mine = plan[-1][1]
            if not swap:
                own = pltpu.make_async_copy(acc[i].at[mine], outs[i].at[mine], local_sem.at[i])
                own.start()
                started[i].append([own])
                return
            copies = []
            for j, (_, target) in enumerate(group):
                copy = remote(
                    acc[i].at[mine, target],
                    outs[i].at[mine, me],
                    swap_send.at[i, j],
                    swap_recv.at[i, j],
                    "shard",
                    target,
                )
                copy.start()
                copies.append(copy)
            own = pltpu.make_async_copy(acc[i].at[mine, me], outs[i].at[mine, me], local_sem.at[i])
            own.start()
            started[i].append(copies + [own])
        else:
            bit, kept, _, length = plan[2 * steps - k]
            region = outs[i].at[pl.ds(kept, length)]
            copy = remote(
                region, region, send.at[i, k - 1], recv.at[i, k - 1], "rep", flip(rep, bit)
            )
            copy.start()
            started[i].append([copy])

    def finish(i, k):
        copies = started[i][k]
        if k < steps:
            copies[0].wait_recv()
            _, kept, _, length = plans[i][k]
            source = ins[i] if k == 0 else acc[i]

            @pl.loop(0, length)
            def _(p):
                acc[i][kept + p] = (
                    source[kept + p].astype(jnp.float32) + box[i][length + p].astype(jnp.float32)
                ).astype(jnp.bfloat16)
        elif k == steps:
            for copy in copies:
                copy.wait()
        else:
            copies[0].wait_recv()

    for i in range(total):
        begin(i, 0)
    for k in range(2 * steps + 1):
        for i in range(total):
            finish(i, k)
            if k < 2 * steps:
                begin(i, k + 1)
    for i in range(total):
        for k in range(2 * steps + 1):
            if k != steps:
                started[i][k][0].wait_send()


def sum_over_rep(collective, arrays, swaps, orders):
    total = len(arrays)
    steps = len(orders[0])
    streams = tuple(zip(orders, swaps))
    return pl.pallas_call(
        functools.partial(sum_kernel, streams),
        out_shape=tuple(jax.ShapeDtypeStruct(a.shape, a.dtype) for a in arrays),
        in_specs=[VMEM] * total,
        out_specs=tuple([VMEM] * total),
        scratch_shapes=[pltpu.VMEM(a.shape, a.dtype) for a in arrays]
        + [pltpu.VMEM(a.shape, a.dtype) for a in arrays]
        + [
            pltpu.SemaphoreType.DMA((total, 2 * steps)),
            pltpu.SemaphoreType.DMA((total, 2 * steps)),
            pltpu.SemaphoreType.DMA((total, 3)),
            pltpu.SemaphoreType.DMA((total, 3)),
            pltpu.SemaphoreType.DMA((total,)),
        ],
        compiler_params=pltpu.CompilerParams(collective_id=collective, has_side_effects=True),
    )(*arrays)


def pieces(flat, n_rep):
    size = flat.shape[-1]
    rows = -(-size // (n_rep * LANES))
    rows = -(-rows // 16) * 16
    room = n_rep * rows * LANES
    flat = jnp.pad(flat, [(0, 0)] * (flat.ndim - 1) + [(0, room - size)])
    split = flat.reshape(flat.shape[:-1] + (n_rep, rows, LANES)).astype(jnp.bfloat16)
    return jnp.moveaxis(split, -3, 0)


def whole(split, size):
    joined = jnp.moveaxis(split, 0, -3)
    return joined.reshape(joined.shape[:-3] + (-1,))[..., :size].astype(jnp.float32)


def local(
    n_shard, n_rep, tokens, gain_one, qkv_weight, out_weight, gain_two, in_weight, down_weight,
    grad_output
):
    tok_dev, width = tokens.shape[1:]
    part = width // n_shard
    heads = part // HEAD_DIM
    hidden = down_weight.shape[0]
    count = tok_dev * n_shard
    scale = HEAD_DIM ** (-0.5)
    f32, b16 = jnp.float32, jnp.bfloat16
    own_tokens = tokens.reshape(tok_dev, width)
    own_grad = grad_output.reshape(tok_dev, width)

    def column_blocks(weight, kinds):
        size = weight.shape[1] // (kinds * n_shard)
        blocks = weight.reshape(part, kinds, n_shard, size).transpose(2, 0, 1, 3)
        return blocks.reshape(n_shard, part, kinds * size)

    gains = jnp.pad(jnp.stack([gain_one, gain_two]), ((0, 14), (0, -part % LANES)))
    all_tokens, all_gains, all_grad, my_qkv, my_in = gather(
        0,
        (own_tokens, gains, own_grad),
        (column_blocks(qkv_weight, 3), column_blocks(in_weight, 2)),
        n_shard,
    )
    full_g1 = all_gains[:, 0, :part].reshape(width)
    full_g2 = all_gains[:, 1, :part].reshape(width)
    my_qkv = my_qkv.reshape(width, 3 * part)
    my_in = my_in.reshape(width, 2 * hidden)
    grad_b = all_grad.reshape(count, width)

    inputs = own_tokens.astype(f32)
    normed_one, inverse_one, _ = layer_norm(inputs, full_g1)
    hidden_one = layer_norm(all_tokens.reshape(count, width).astype(f32), full_g1)[2].astype(b16)
    projected = jnp.dot(hidden_one, my_qkv, preferred_element_type=f32)
    cosine, sine = rotary_tables(count, HEAD_DIM)
    split = projected.reshape(count, 3, heads, HEAD_DIM).transpose(1, 2, 0, 3)
    queries, key_raw = split[0], split[1]
    query_rot = (queries * cosine + rotate_half(queries) * sine).astype(b16)
    key_rot = (key_raw * cosine + rotate_half(key_raw) * sine).astype(b16)
    values = split[2].astype(b16)
    scores = jnp.einsum("hqd,hkd->hqk", query_rot, key_rot, preferred_element_type=f32) * scale
    maxima = jnp.max(scores, axis=-1, keepdims=True)
    expo = jnp.exp(scores - maxima)
    totals = jnp.sum(expo, axis=-1, keepdims=True)
    accum = jnp.einsum("hqk,hkd->hqd", expo.astype(b16), values, preferred_element_type=f32)
    att_heads = (accum / totals).astype(b16)
    attended = att_heads.transpose(1, 0, 2).reshape(count, part)
    partial = jnp.dot(attended, out_weight, preferred_element_type=f32).astype(b16)
    (mixed,) = scatter(1, (partial.reshape(n_shard, tok_dev, width),))
    resid = inputs + mixed
    normed_two, inverse_two, scaled_two = layer_norm(resid, full_g2)
    (hidden_two,) = gather(2, (scaled_two.astype(b16),), (), n_shard)
    hidden_two = hidden_two.reshape(count, width)
    upper = jnp.dot(hidden_two, my_in, preferred_element_type=f32)
    inner, gate_half = upper[:, :hidden], upper[:, hidden:]
    gelu_value, gelu_slope = gelu_pair(inner)
    act = (gelu_value * gate_half).astype(b16)
    down_part = jnp.dot(act, down_weight, preferred_element_type=f32).astype(b16)
    grad_down = outer_sum(act, grad_b)
    grad_act = times_transposed(grad_b, down_weight)
    grad_upper = jnp.concatenate(
        [grad_act * gate_half * gelu_slope, grad_act * gelu_value], axis=-1
    ).astype(b16)
    grad_in = outer_sum(hidden_two, grad_upper)
    h2_part = times_transposed(grad_upper, my_in).astype(b16)
    down_sum, grad_h2 = scatter(
        3, (down_part.reshape(n_shard, tok_dev, width), h2_part.reshape(n_shard, tok_dev, width))
    )
    output = (resid + down_sum).astype(b16)
    norm_grad_two, grad_gain_two = norm_backward(grad_h2, normed_two, inverse_two, full_g2)
    grad_resid = own_grad.astype(f32) + norm_grad_two
    (resid_b,) = gather(4, (grad_resid.astype(b16),), (), n_shard)
    resid_b = resid_b.reshape(count, width)
    grad_out = outer_sum(attended, resid_b)
    grad_att = times_transposed(resid_b, out_weight).astype(b16)
    grad_heads = grad_att.reshape(count, heads, HEAD_DIM).transpose(1, 0, 2)
    delta = jnp.sum(grad_heads.astype(f32) * att_heads.astype(f32), axis=-1, keepdims=True)
    probs = expo / totals
    grad_value = jnp.einsum(
        "hqk,hqd->khd", probs.astype(b16), grad_heads, preferred_element_type=f32
    )
    grad_probs = jnp.einsum("hqd,hkd->hqk", grad_heads, values, preferred_element_type=f32)
    grad_scores = (probs * (grad_probs - delta) * scale).astype(b16)
    grad_qr = jnp.einsum("hqk,hkd->hqd", grad_scores, key_rot, preferred_element_type=f32)
    grad_kr = jnp.einsum("hqk,hqd->hkd", grad_scores, query_rot, preferred_element_type=f32)
    grad_q = (grad_qr * cosine - rotate_half(grad_qr) * sine).transpose(1, 0, 2)
    grad_k = (grad_kr * cosine - rotate_half(grad_kr) * sine).transpose(1, 0, 2)
    grad_projected = jnp.concatenate(
        [g.reshape(count, part) for g in (grad_q, grad_k, grad_value)], axis=-1
    ).astype(b16)
    grad_qkv = outer_sum(hidden_one, grad_projected)
    h1_part = times_transposed(grad_projected, my_qkv).astype(b16)
    (grad_h1,) = scatter(5, (h1_part.reshape(n_shard, tok_dev, width),))
    norm_grad_one, grad_gain_one = norm_backward(grad_h1, normed_one, inverse_one, full_g1)
    grad_tokens = grad_resid + norm_grad_one

    def with_gain(grad, gain):
        return jnp.concatenate([grad.reshape(n_shard, -1), gain.reshape(n_shard, -1)], axis=-1)

    low_first = tuple(1 << i for i in range(n_rep.bit_length() - 1))
    low_last = low_first[1:] + low_first[:1]
    plain = jnp.concatenate([grad_out.reshape(-1), grad_down.reshape(-1)])
    wide = part * 3 * part
    tall = part * 2 * hidden
    summed_plain, summed_in, summed_qkv = sum_over_rep(
        6,
        (
            pieces(plain, n_rep),
            pieces(with_gain(grad_in, grad_gain_two), n_rep),
            pieces(with_gain(grad_qkv, grad_gain_one), n_rep),
        ),
        (False, True, True),
        (low_first, low_last, low_first),
    )
    sum_plain = whole(summed_plain, plain.shape[0])
    sum_in = whole(summed_in, tall + part)
    sum_qkv = whole(summed_qkv, wide + part)

    def rows(blocks, kinds, size):
        blocks = blocks.reshape(n_shard, part, kinds, size).transpose(1, 2, 0, 3)
        return blocks.reshape(part, kinds * n_shard * size)

    return (
        output.reshape(1, tok_dev, width),
        grad_tokens.reshape(1, tok_dev, width),
        jnp.sum(sum_qkv[:, wide:], axis=0),
        rows(sum_qkv[:, :wide], 3, part),
        sum_plain[: part * width].reshape(part, width),
        jnp.sum(sum_in[:, tall:], axis=0),
        rows(sum_in[:, :tall], 2, hidden),
        sum_plain[part * width :].reshape(hidden, width),
    )


def solution(mesh):
    in_specs = (
        P("rep", "shard", None),
        P("shard"),
        P("shard", None),
        P("shard", None),
        P("shard"),
        P("shard", None),
        P("shard", None),
        P("rep", "shard", None),
    )
    out_specs = (
        P("rep", "shard", None),
        P("rep", "shard", None),
        P("shard"),
        P("shard", None),
        P("shard", None),
        P("shard"),
        P("shard", None),
        P("shard", None),
    )
    body = functools.partial(local, mesh.shape["shard"], mesh.shape["rep"])
    return jax.shard_map(body, mesh=mesh, in_specs=in_specs, out_specs=out_specs, check_vma=False)
```

```python
import functools

import jax
import jax.numpy as jnp
from jax import lax
from jax.experimental import pallas as pl
from jax.experimental.pallas import tpu as pltpu
from jax.sharding import PartitionSpec as P

HEAD_DIM = 64
EPSILON = 1e-05
THETA = 160000.0
SQRT_HALF = 0.7071067811865476
INV_SQRT_TAU = 0.3989422804014327
MESH_ID = pl.DeviceIdType.MESH
LANES = 128
VMEM = pl.BlockSpec(memory_space=pltpu.VMEM)


def layer_norm(values, gain):
    mean_row = jnp.mean(values, axis=-1, keepdims=True)
    centred = values - mean_row
    variance = jnp.mean(centred * centred, axis=-1, keepdims=True)
    inverse = lax.rsqrt(variance + EPSILON)
    normed = centred * inverse
    return (normed, inverse, normed * gain.astype(jnp.float32))


def norm_backward(grad_out, normed, inverse, gain):
    grad_normed = grad_out * gain.astype(jnp.float32)
    gain_grad = jnp.sum(grad_out * normed, axis=0)
    first = jnp.mean(grad_normed, axis=-1, keepdims=True)
    second = jnp.mean(grad_normed * normed, axis=-1, keepdims=True)
    return (inverse * (grad_normed - first - normed * second), gain_grad)


def rotary_tables(count, head_dim):
    half = head_dim // 2
    positions = jnp.arange(count, dtype=jnp.int32)
    freq = THETA ** (-jnp.arange(half, dtype=jnp.float32) * 2.0 / head_dim)
    angles = positions.astype(jnp.float32)[:, None] * freq[None, :]
    angles = jnp.concatenate([angles, angles], axis=-1)
    return (jnp.cos(angles)[None], jnp.sin(angles)[None])


def rotate_half(values):
    half = values.shape[-1] // 2
    return jnp.concatenate([-values[..., half:], values[..., :half]], axis=-1)


def gelu_pair(inner):
    cdf = 0.5 * (1.0 + jax.scipy.special.erf(inner * SQRT_HALF))
    return (inner * cdf, cdf + inner * jnp.exp(-0.5 * inner * inner) * INV_SQRT_TAU)


def outer_sum(left, right):
    return lax.dot_general(
        left, right, (((0,), (0,)), ((), ())), preferred_element_type=jnp.float32
    )


def times_transposed(left, weight):
    return lax.dot_general(
        left, weight, (((1,), (1,)), ((), ())), preferred_element_type=jnp.float32
    )


def flip(index, bit):
    return index + bit * (1 - 2 * ((index // bit) % 2))


def remote(src, dst, send, recv, axis, target):
    return pltpu.make_async_remote_copy(
        src_ref=src,
        dst_ref=dst,
        send_sem=send,
        recv_sem=recv,
        device_id={axis: target},
        device_id_type=MESH_ID,
    )


def greet(partners):
    barrier = pltpu.get_barrier_semaphore()
    for axis, target in partners:
        pl.semaphore_signal(barrier, inc=1, device_id={axis: target}, device_id_type=MESH_ID)
    pl.semaphore_wait(barrier, len(partners))


def shard_partners(me):
    return [("shard", flip(me, 1)), ("shard", flip(me, 2)), ("shard", flip(flip(me, 1), 2))]


def gather_kernel(gathered, kinds, *refs):
    total = gathered + len(kinds)
    ins, outs = refs[:total], refs[total : 2 * total]
    packed = refs[2 * total : 2 * total + len(kinds)]
    send, recv, local_sem = refs[2 * total + len(kinds) :]
    me = lax.axis_index("shard")
    partners = shard_partners(me)
    greet(partners)
    (_, core), (_, chip), (_, diagonal) = partners
    pending = []
    sent = []
    for i in range(gathered):
        far = remote(ins[i], outs[i].at[me], send.at[i, 0], recv.at[i, 0], "shard", chip)
        far.start()
        near = remote(ins[i], outs[i].at[me], send.at[i, 1], recv.at[i, 1], "shard", core)
        near.start()
        own = pltpu.make_async_copy(ins[i], outs[i].at[me], local_sem.at[i])
        own.start()
        pending.append((far, near, own))
    for i in range(gathered, total):
        source, buffer, kind_count = ins[i], packed[i - gathered], kinds[i - gathered]
        blocks, _, columns = buffer.shape
        size = columns // kind_count
        for j in range(blocks):
            for kind in range(kind_count):
                start = (kind * blocks + j) * size
                buffer[j, :, kind * size : (kind + 1) * size] = source[:, start : start + size]
        copies = []
        for k, target in enumerate((chip, diagonal, core)):
            copy = remote(
                buffer.at[target], outs[i].at[me], send.at[i, k], recv.at[i, k], "shard", target
            )
            copy.start()
            copies.append(copy)
        own = pltpu.make_async_copy(buffer.at[me], outs[i].at[me], local_sem.at[i])
        own.start()
        sent.append((copies, own))
    for i in range(gathered):
        pending[i][0].wait_recv()
        relay = remote(
            outs[i].at[chip], outs[i].at[chip], send.at[i, 2], recv.at[i, 2], "shard", core
        )
        relay.start()
        pending[i] = pending[i] + (relay,)
    for far, near, own, relay in pending:
        far.wait_send()
        near.wait()
        own.wait()
        relay.wait()
    for copies, own in sent:
        for copy in copies:
            copy.wait()
        own.wait()


def gather(collective, gathered, swapped, kinds, n_shard):
    arrays = tuple(gathered) + tuple(swapped)
    shapes = [jax.ShapeDtypeStruct((n_shard,) + a.shape, a.dtype) for a in gathered]
    blocks = [
        jax.ShapeDtypeStruct((n_shard, a.shape[0], a.shape[1] // n_shard), a.dtype)
        for a in swapped
    ]
    return pl.pallas_call(
        functools.partial(gather_kernel, len(gathered), tuple(kinds)),
        out_shape=tuple(shapes + blocks),
        in_specs=[VMEM] * len(arrays),
        out_specs=tuple([VMEM] * len(arrays)),
        scratch_shapes=[pltpu.VMEM(b.shape, b.dtype) for b in blocks]
        + [
            pltpu.SemaphoreType.DMA((len(arrays), 3)),
            pltpu.SemaphoreType.DMA((len(arrays), 3)),
            pltpu.SemaphoreType.DMA((len(arrays),)),
        ],
        compiler_params=pltpu.CompilerParams(collective_id=collective, has_side_effects=True),
    )(*arrays)


def scatter_kernel(total, *refs):
    ins, outs = refs[:total], refs[total : 2 * total]
    near_buf, out_buf, far_buf, send, recv = refs[2 * total :]
    me = lax.axis_index("shard")
    partners = shard_partners(me)[:2]
    greet(partners)
    (_, core), (_, chip) = partners
    diagonal = flip(core, 2)
    first, second, third = [], [], []
    for i in range(total):
        a = remote(
            ins[i].at[diagonal], near_buf.at[i, 0], send.at[i, 0], recv.at[i, 0], "shard", core
        )
        a.start()
        b = remote(ins[i].at[core], near_buf.at[i, 1], send.at[i, 1], recv.at[i, 1], "shard", core)
        b.start()
        first.append(a)
        second.append(b)
    for i in range(total):
        first[i].wait_recv()
        out_buf[i] = (
            ins[i][chip].astype(jnp.float32) + near_buf[i, 0].astype(jnp.float32)
        ).astype(jnp.bfloat16)
        c = remote(out_buf.at[i], far_buf.at[i], send.at[i, 2], recv.at[i, 2], "shard", chip)
        c.start()
        third.append(c)
    for i in range(total):
        second[i].wait_recv()
        outs[i][...] = ins[i][me].astype(jnp.float32) + near_buf[i, 1].astype(jnp.float32)
    for i in range(total):
        third[i].wait_recv()
        outs[i][...] += far_buf[i].astype(jnp.float32)
    for i in range(total):
        first[i].wait_send()
        second[i].wait_send()
        third[i].wait_send()


def scatter(collective, arrays):
    total = len(arrays)
    block = arrays[0].shape[1:]
    return pl.pallas_call(
        functools.partial(scatter_kernel, total),
        out_shape=tuple([jax.ShapeDtypeStruct(block, jnp.float32)] * total),
        in_specs=[VMEM] * total,
        out_specs=tuple([VMEM] * total),
        scratch_shapes=[
            pltpu.VMEM((total, 2) + block, jnp.bfloat16),
            pltpu.VMEM((total,) + block, jnp.bfloat16),
            pltpu.VMEM((total,) + block, jnp.bfloat16),
            pltpu.SemaphoreType.DMA((total, 3)),
            pltpu.SemaphoreType.DMA((total, 3)),
        ],
        compiler_params=pltpu.CompilerParams(collective_id=collective, has_side_effects=True),
    )(*arrays)


def halves(order, me):
    length = 1 << len(order)
    offset = 0
    plan = []
    for bit in order:
        length //= 2
        side = (me // bit) % 2
        plan.append((bit, offset + side * length, offset + (1 - side) * length, length))
        offset = offset + side * length
    return plan


class Stream:
    def __init__(self, buffer, base, rows, order, swap):
        self.buffer, self.base, self.rows, self.order, self.swap = buffer, base, rows, order, swap


def streams_of(buffer, rows, n_rep, swap):
    tiles = -(-rows // (16 * n_rep))
    low_first = tuple(1 << i for i in range(n_rep.bit_length() - 1))
    orders = (low_first, low_first[1::-1] + low_first[2:])
    streams = []
    base = 0
    for share, order in zip((tiles - tiles // 2, tiles // 2), orders):
        if share:
            streams.append(Stream(buffer, base, 16 * share, order, swap))
            base += 16 * share * n_rep
    return streams, base


class RepSum:
    def __init__(self, streams, acc, box, res, sems):
        self.streams, self.acc, self.box, self.res = streams, acc, box, res
        self.send, self.recv, self.swap_send, self.swap_recv, self.local_sem = sems
        self.rep = lax.axis_index("rep")
        self.me = lax.axis_index("shard")
        self.group = shard_partners(self.me)
        self.steps = len(streams[0].order)
        self.plans = [halves(stream.order, self.rep) for stream in streams]
        self.started = [[] for _ in streams]

    def at(self, ref, i, piece, length, lead=None):
        stream = self.streams[i]
        start = stream.base + piece * stream.rows
        if not isinstance(start, int):
            start = pl.multiple_of(start, 16)
        rows = pl.ds(start, length * stream.rows)
        if not stream.swap:
            return ref.at[rows]
        return ref.at[slice(None) if lead is None else lead, rows]

    def begin(self, i, k):
        stream, plan, steps = self.streams[i], self.plans[i], self.steps
        acc, box, res = (refs[stream.buffer] for refs in (self.acc, self.box, self.res))
        if k < steps:
            bit, _, sent, length = plan[k]
            copies = [
                remote(
                    self.at(acc, i, sent, length),
                    self.at(box, i, length, length),
                    self.send.at[i, k],
                    self.recv.at[i, k],
                    "rep",
                    flip(self.rep, bit),
                )
            ]
        elif k == steps:
            mine = plan[-1][1]
            if not stream.swap:
                copies = [
                    pltpu.make_async_copy(
                        self.at(acc, i, mine, 1), self.at(res, i, mine, 1), self.local_sem.at[i]
                    )
                ]
            else:
                target_block = self.at(res, i, mine, 1, self.me)
                copies = [
                    remote(
                        self.at(acc, i, mine, 1, target),
                        target_block,
                        self.swap_send.at[i, j],
                        self.swap_recv.at[i, j],
                        "shard",
                        target,
                    )
                    for j, (_, target) in enumerate(self.group)
                ]
                copies.append(
                    pltpu.make_async_copy(
                        self.at(acc, i, mine, 1, self.me), target_block, self.local_sem.at[i]
                    )
                )
        else:
            bit, kept, _, length = plan[2 * steps - k]
            region = self.at(res, i, kept, length)
            copies = [
                remote(
                    region,
                    region,
                    self.send.at[i, k - 1],
                    self.recv.at[i, k - 1],
                    "rep",
                    flip(self.rep, bit),
                )
            ]
        for copy in copies:
            copy.start()
        self.started[i].append(copies)

    def finish(self, i, k):
        copies, stream = self.started[i][k], self.streams[i]
        if k == self.steps:
            for copy in copies:
                copy.wait()
            return
        copies[0].wait_recv()
        if k > self.steps:
            return
        acc, box = self.acc[stream.buffer], self.box[stream.buffer]
        _, kept, _, length = self.plans[i][k]
        blocks = range(acc.shape[0]) if stream.swap else (None,)

        @pl.loop(0, length * stream.rows // 16)
        def _(p):
            to = pl.ds(pl.multiple_of(stream.base + kept * stream.rows + 16 * p, 16), 16)
            of = pl.ds(pl.multiple_of(stream.base + length * stream.rows + 16 * p, 16), 16)
            for block in blocks:
                x, y = ((to,), (of,)) if block is None else ((block, to), (block, of))
                acc[x] = (acc[x].astype(jnp.float32) + box[y].astype(jnp.float32)).astype(
                    jnp.bfloat16
                )

    def begin_all(self, chosen):
        for i in chosen:
            self.begin(i, 0)

    def step(self, chosen, k):
        for i in chosen:
            self.finish(i, k)
            if k < 2 * self.steps:
                self.begin(i, k + 1)

    def close(self, chosen):
        for i in chosen:
            for k in range(2 * self.steps + 1):
                if k != self.steps:
                    self.started[i][k][0].wait_send()


def pack_columns(source, target, gain):
    blocks, rows, columns = source.shape
    full, rest = divmod(columns, LANES)
    for s in range(blocks):
        for j in range(full):
            target[s, j * rows : (j + 1) * rows] = source[s, :, j * LANES : (j + 1) * LANES]
        at = full * rows
        if rest:
            half = rows // 2
            target[s, at : at + half, :rest] = source[s, :half, full * LANES :]
            target[s, at : at + half, rest:] = source[s, half:, full * LANES :]
            at += half
        target[s, at : at + 16] = gain[s]
        if at + 16 < target.shape[1]:
            target[s, at + 16 :] = jnp.zeros((target.shape[1] - at - 16, LANES), target.dtype)


def unpack_columns(source, out, gain_out, kinds):
    blocks = source.shape[0]
    rows, width = out.shape
    columns = width // blocks
    size = columns // kinds
    full, rest = divmod(columns, LANES)
    half = rows // 2
    at = full * rows
    gain = jnp.zeros((16, LANES), jnp.float32)
    for t in range(blocks):
        parts = [source[t, j * rows : (j + 1) * rows] for j in range(full)]
        end = at
        if rest:
            tail = source[t, at : at + half]
            parts.append(jnp.concatenate([tail[:, :rest], tail[:, rest:]], axis=0))
            end += half
        block = jnp.concatenate([p.astype(jnp.float32) for p in parts], axis=1)
        gain += source[t, end : end + 16].astype(jnp.float32)
        for kind in range(kinds):
            start = (kind * blocks + t) * size
            out[:, start : start + size] = block[:, kind * size : (kind + 1) * size]
    gain_out[...] = gain


def pack_rows(sources, target):
    tall = sum(source.shape[0] for source in sources)
    at = 0
    for source in sources:
        rows = source.shape[0]
        for j in range(source.shape[1] // LANES):
            target[j * tall + at : j * tall + at + rows] = source[:, j * LANES : (j + 1) * LANES]
        at += rows
    end = tall * sources[0].shape[1] // LANES
    if end < target.shape[0]:
        target[end:] = jnp.zeros((target.shape[0] - end, LANES), target.dtype)


def unpack_rows(source, outs):
    tall = sum(out.shape[0] for out in outs)
    at = 0
    for out in outs:
        rows = out.shape[0]
        for j in range(out.shape[1] // LANES):
            out[:, j * LANES : (j + 1) * LANES] = source[
                j * tall + at : j * tall + at + rows
            ].astype(jnp.float32)
        at += rows


def column_rows(shape):
    _, rows, columns = shape
    return rows * columns // LANES + 16


def sum_kernel(streams, qkv, gain1, win, gain2, gout, gdown, *refs):
    o_qkv, o_gain1, o_in, o_gain2, o_out, o_down = refs[:6]
    acc, box, res = refs[6:9], refs[9:12], refs[12:15]
    pack_rows((gout, gdown), acc[0])
    pack_columns(win, acc[1], gain2)
    pack_columns(qkv, acc[2], gain1)
    rep_sum = RepSum(streams, acc, box, res, refs[15:])
    bits = sorted(streams[0].order)
    greet([("rep", flip(rep_sum.rep, bit)) for bit in bits] + rep_sum.group)
    chosen = range(len(streams))
    rep_sum.begin_all(chosen)
    for k in range(2 * rep_sum.steps + 1):
        rep_sum.step(chosen, k)
    unpack_rows(res[0], (o_out, o_down))
    unpack_columns(res[1], o_in, o_gain2, 2)
    unpack_columns(res[2], o_qkv, o_gain1, 3)
    rep_sum.close(chosen)


def sum_over_rep(collective, n_rep, qkv, gain1, win, gain2, gout, gdown):
    b16, f32 = jnp.bfloat16, jnp.float32
    n_shard, part, columns = qkv.shape
    width = columns * n_shard
    plain_rows = (gout.shape[0] + gdown.shape[0]) * gout.shape[1] // LANES
    streams, shapes = [], []
    for i, (rows, swap) in enumerate(
        ((plain_rows, False), (column_rows(win.shape), True), (column_rows(qkv.shape), True))
    ):
        more, padded = streams_of(i, rows, n_rep, swap)
        streams += more
        shapes.append((n_shard, padded, LANES) if swap else (padded, LANES))
    steps = len(streams[0].order)
    count = len(streams)
    outs = [(part, width), (16, LANES), (part, win.shape[2] * n_shard), (16, LANES)]
    outs += [gout.shape, gdown.shape]
    return pl.pallas_call(
        functools.partial(sum_kernel, streams),
        out_shape=tuple(jax.ShapeDtypeStruct(shape, f32) for shape in outs),
        in_specs=[VMEM] * 6,
        out_specs=tuple([VMEM] * 6),
        scratch_shapes=[pltpu.VMEM(shape, b16) for shape in shapes * 3]
        + [
            pltpu.SemaphoreType.DMA((count, 2 * steps)),
            pltpu.SemaphoreType.DMA((count, 2 * steps)),
            pltpu.SemaphoreType.DMA((count, 3)),
            pltpu.SemaphoreType.DMA((count, 3)),
            pltpu.SemaphoreType.DMA((count,)),
        ],
        compiler_params=pltpu.CompilerParams(collective_id=collective, has_side_effects=True),
    )(qkv, gain1, win, gain2, gout, gdown)


def local(
    n_shard, n_rep, tokens, gain_one, qkv_weight, out_weight, gain_two, in_weight, down_weight,
    grad_output
):
    tok_dev, width = tokens.shape[1:]
    part = width // n_shard
    heads = part // HEAD_DIM
    hidden = down_weight.shape[0]
    count = tok_dev * n_shard
    scale = HEAD_DIM ** (-0.5)
    f32, b16 = jnp.float32, jnp.bfloat16
    own_tokens = tokens.reshape(tok_dev, width)
    own_grad = grad_output.reshape(tok_dev, width)

    all_tokens, all_g1, all_g2, all_grad, my_qkv, my_in = gather(
        0,
        (own_tokens, gain_one.reshape(1, part), gain_two.reshape(1, part), own_grad),
        (qkv_weight, in_weight),
        (3, 2),
        n_shard,
    )
    full_g1 = all_g1.reshape(width)
    full_g2 = all_g2.reshape(width)
    my_qkv = my_qkv.reshape(width, 3 * part)
    my_in = my_in.reshape(width, 2 * hidden)
    grad_b = all_grad.reshape(count, width)

    inputs = own_tokens.astype(f32)
    normed_one, inverse_one, _ = layer_norm(inputs, full_g1)
    hidden_one = layer_norm(all_tokens.reshape(count, width).astype(f32), full_g1)[2].astype(b16)
    projected = jnp.dot(hidden_one, my_qkv, preferred_element_type=f32)
    cosine, sine = rotary_tables(count, HEAD_DIM)
    split = projected.reshape(count, 3, heads, HEAD_DIM).transpose(1, 2, 0, 3)
    queries, key_raw = split[0], split[1]
    query_rot = (queries * cosine + rotate_half(queries) * sine).astype(b16)
    key_rot = (key_raw * cosine + rotate_half(key_raw) * sine).astype(b16)
    values = split[2].astype(b16)
    scores = jnp.einsum("hqd,hkd->hqk", query_rot, key_rot, preferred_element_type=f32) * scale
    maxima = jnp.max(scores, axis=-1, keepdims=True)
    expo = jnp.exp(scores - maxima)
    totals = jnp.sum(expo, axis=-1, keepdims=True)
    accum = jnp.einsum("hqk,hkd->hqd", expo.astype(b16), values, preferred_element_type=f32)
    att_heads = (accum / totals).astype(b16)
    attended = att_heads.transpose(1, 0, 2).reshape(count, part)
    partial = jnp.dot(attended, out_weight, preferred_element_type=f32).astype(b16)
    (mixed,) = scatter(1, (partial.reshape(n_shard, tok_dev, width),))
    resid = inputs + mixed
    normed_two, inverse_two, scaled_two = layer_norm(resid, full_g2)
    (hidden_two,) = gather(2, (scaled_two.astype(b16),), (), (), n_shard)
    hidden_two = hidden_two.reshape(count, width)
    upper = jnp.dot(hidden_two, my_in, preferred_element_type=f32)
    inner, gate_half = upper[:, :hidden], upper[:, hidden:]
    gelu_value, gelu_slope = gelu_pair(inner)
    act = (gelu_value * gate_half).astype(b16)
    down_part = jnp.dot(act, down_weight, preferred_element_type=f32).astype(b16)
    grad_down = outer_sum(act, grad_b)
    grad_act = times_transposed(grad_b, down_weight)
    grad_upper = jnp.concatenate(
        [grad_act * gate_half * gelu_slope, grad_act * gelu_value], axis=-1
    ).astype(b16)
    grad_in = outer_sum(hidden_two, grad_upper)
    h2_part = times_transposed(grad_upper, my_in).astype(b16)
    down_sum, grad_h2 = scatter(
        3, (down_part.reshape(n_shard, tok_dev, width), h2_part.reshape(n_shard, tok_dev, width))
    )
    output = (resid + down_sum).astype(b16)
    norm_grad_two, grad_gain_two = norm_backward(grad_h2, normed_two, inverse_two, full_g2)
    grad_resid = own_grad.astype(f32) + norm_grad_two
    (resid_b,) = gather(4, (grad_resid.astype(b16),), (), (), n_shard)
    resid_b = resid_b.reshape(count, width)
    grad_out = outer_sum(attended, resid_b)
    grad_att = times_transposed(resid_b, out_weight).astype(b16)
    grad_heads = grad_att.reshape(count, heads, HEAD_DIM).transpose(1, 0, 2)
    delta = jnp.sum(grad_heads.astype(f32) * att_heads.astype(f32), axis=-1, keepdims=True)
    probs = expo / totals
    grad_value = jnp.einsum(
        "hqk,hqd->khd", probs.astype(b16), grad_heads, preferred_element_type=f32
    )
    grad_probs = jnp.einsum("hqd,hkd->hqk", grad_heads, values, preferred_element_type=f32)
    grad_scores = (probs * (grad_probs - delta) * scale).astype(b16)
    grad_qr = jnp.einsum("hqk,hkd->hqd", grad_scores, key_rot, preferred_element_type=f32)
    grad_kr = jnp.einsum("hqk,hqd->hkd", grad_scores, query_rot, preferred_element_type=f32)
    grad_q = (grad_qr * cosine - rotate_half(grad_qr) * sine).transpose(1, 0, 2)
    grad_k = (grad_kr * cosine - rotate_half(grad_kr) * sine).transpose(1, 0, 2)
    grad_projected = jnp.concatenate(
        [g.reshape(count, part) for g in (grad_q, grad_k, grad_value)], axis=-1
    ).astype(b16)
    grad_qkv = outer_sum(hidden_one, grad_projected)
    h1_part = times_transposed(grad_projected, my_qkv).astype(b16)
    (grad_h1,) = scatter(5, (h1_part.reshape(n_shard, tok_dev, width),))
    norm_grad_one, grad_gain_one = norm_backward(grad_h1, normed_one, inverse_one, full_g1)
    grad_tokens = grad_resid + norm_grad_one

    def gain_rows(gain):
        room = -part % LANES
        rows = jnp.pad(gain.reshape(n_shard, part), ((0, 0), (0, room)))
        rows = rows.reshape(n_shard, -1, LANES)
        return jnp.pad(rows, ((0, 0), (0, 16 - rows.shape[1]), (0, 0))).astype(b16)

    sum_qkv, sum_g1, sum_in, sum_g2, sum_out, sum_down = sum_over_rep(
        6,
        n_rep,
        grad_qkv.astype(b16).reshape(n_shard, part, -1),
        gain_rows(grad_gain_one),
        grad_in.astype(b16).reshape(n_shard, part, -1),
        gain_rows(grad_gain_two),
        grad_out.astype(b16),
        grad_down.astype(b16),
    )
    return (
        output.reshape(1, tok_dev, width),
        grad_tokens.reshape(1, tok_dev, width),
        sum_g1.reshape(-1)[:part],
        sum_qkv,
        sum_out,
        sum_g2.reshape(-1)[:part],
        sum_in,
        sum_down,
    )


def solution(mesh):
    in_specs = (
        P("rep", "shard", None),
        P("shard"),
        P("shard", None),
        P("shard", None),
        P("shard"),
        P("shard", None),
        P("shard", None),
        P("rep", "shard", None),
    )
    out_specs = (
        P("rep", "shard", None),
        P("rep", "shard", None),
        P("shard"),
        P("shard", None),
        P("shard", None),
        P("shard"),
        P("shard", None),
        P("shard", None),
    )
    body = functools.partial(local, mesh.shape["shard"], mesh.shape["rep"])
    return jax.shard_map(body, mesh=mesh, in_specs=in_specs, out_specs=out_specs, check_vma=False)
```

```python
import functools

import jax
import jax.numpy as jnp
from jax import lax
from jax.experimental import pallas as pl
from jax.experimental.pallas import tpu as pltpu
from jax.sharding import PartitionSpec as P

HEAD_DIM = 64
EPSILON = 1e-05
THETA = 160000.0
SQRT_HALF = 0.7071067811865476
INV_SQRT_TAU = 0.3989422804014327
MESH_ID = pl.DeviceIdType.MESH
LANES = 128
VMEM = pl.BlockSpec(memory_space=pltpu.VMEM)


def layer_norm(values, gain):
    mean_row = jnp.mean(values, axis=-1, keepdims=True)
    centred = values - mean_row
    variance = jnp.mean(centred * centred, axis=-1, keepdims=True)
    inverse = lax.rsqrt(variance + EPSILON)
    normed = centred * inverse
    return (normed, inverse, normed * gain.astype(jnp.float32))


def norm_backward(grad_out, normed, inverse, gain):
    grad_normed = grad_out * gain.astype(jnp.float32)
    gain_grad = jnp.sum(grad_out * normed, axis=0)
    first = jnp.mean(grad_normed, axis=-1, keepdims=True)
    second = jnp.mean(grad_normed * normed, axis=-1, keepdims=True)
    return (inverse * (grad_normed - first - normed * second), gain_grad)


def rotary_tables(count, head_dim):
    half = head_dim // 2
    positions = jnp.arange(count, dtype=jnp.int32)
    freq = THETA ** (-jnp.arange(half, dtype=jnp.float32) * 2.0 / head_dim)
    angles = positions.astype(jnp.float32)[:, None] * freq[None, :]
    angles = jnp.concatenate([angles, angles], axis=-1)
    return (jnp.cos(angles)[None], jnp.sin(angles)[None])


def rotate_half(values):
    half = values.shape[-1] // 2
    return jnp.concatenate([-values[..., half:], values[..., :half]], axis=-1)


def gelu_pair(inner):
    cdf = 0.5 * (1.0 + jax.scipy.special.erf(inner * SQRT_HALF))
    return (inner * cdf, cdf + inner * jnp.exp(-0.5 * inner * inner) * INV_SQRT_TAU)


def outer_sum(left, right):
    return lax.dot_general(
        left, right, (((0,), (0,)), ((), ())), preferred_element_type=jnp.float32
    )


def times_transposed(left, weight):
    return lax.dot_general(
        left, weight, (((1,), (1,)), ((), ())), preferred_element_type=jnp.float32
    )


def flip(index, bit):
    return index + bit * (1 - 2 * ((index // bit) % 2))


def remote(src, dst, send, recv, axis, target):
    return pltpu.make_async_remote_copy(
        src_ref=src,
        dst_ref=dst,
        send_sem=send,
        recv_sem=recv,
        device_id={axis: target},
        device_id_type=MESH_ID,
    )


def greet(partners):
    barrier = pltpu.get_barrier_semaphore()
    for axis, target in partners:
        pl.semaphore_signal(barrier, inc=1, device_id={axis: target}, device_id_type=MESH_ID)
    pl.semaphore_wait(barrier, len(partners))


def shard_partners(me):
    return [("shard", flip(me, 1)), ("shard", flip(me, 2)), ("shard", flip(flip(me, 1), 2))]


def gather_kernel(gathered, kinds, relays, *refs):
    total = gathered + len(kinds)
    ins, outs = refs[:total], refs[total : 2 * total]
    packed = refs[2 * total : 2 * total + len(kinds)]
    send, recv, local_sem = refs[2 * total + len(kinds) :]
    me = lax.axis_index("shard")
    partners = shard_partners(me)
    rep = lax.axis_index("rep")
    bits = [1 << b for b in range(relays)] if kinds else []
    greet(partners + [("rep", flip(rep, bit)) for bit in bits])
    (_, core), (_, chip), (_, diagonal) = partners
    pending = []

    def begin(i):
        far = remote(ins[i], outs[i].at[me], send.at[i, 0], recv.at[i, 0], "shard", chip)
        far.start()
        near = remote(ins[i], outs[i].at[me], send.at[i, 1], recv.at[i, 1], "shard", core)
        near.start()
        own = pltpu.make_async_copy(ins[i], outs[i].at[me], local_sem.at[i])
        own.start()
        pending.append((far, near, own))

    def pass_on(i):
        pending[i][0].wait_recv()
        relay = remote(
            outs[i].at[chip], outs[i].at[chip], send.at[i, 2], recv.at[i, 2], "shard", core
        )
        relay.start()
        pending[i] = pending[i] + (relay,)

    late = gathered - 1 if kinds else gathered
    for i in range(late):
        begin(i)
    shared, whole_copies, own_copies = [], [], []
    for i in range(gathered, total):
        source, buffer, kind_count = ins[i], packed[i - gathered], kinds[i - gathered]
        blocks, tall, columns = buffer.shape
        size = columns // kind_count
        for j in range(blocks):
            for kind in range(kind_count):
                start = (kind * blocks + j) * size
                buffer[j, :, kind * size : (kind + 1) * size] = source[:, start : start + size]
        share = tall >> relays
        rows = pl.ds(pl.multiple_of((rep % (1 << relays)) * share, share), share)
        for k, target in enumerate((chip, diagonal)):
            copy = remote(
                buffer.at[target, rows],
                outs[i].at[me, rows],
                send.at[i, k],
                recv.at[i, k],
                "shard",
                target,
            )
            copy.start()
            shared.append((i, k, target, tall, [copy]))
        copy = remote(
            buffer.at[core], outs[i].at[me], send.at[i, 2], recv.at[i, 2], "shard", core
        )
        copy.start()
        whole_copies.append(copy)
        own = pltpu.make_async_copy(buffer.at[me], outs[i].at[me], local_sem.at[i])
        own.start()
        own_copies.append(own)
    for i in range(late, gathered):
        begin(i)
    for i in range(late):
        pass_on(i)
    for level, bit in enumerate(bits):
        for i, k, target, tall, copies in shared:
            copies[-1].wait_recv()
            length = (tall >> relays) * bit
            first = ((rep % (1 << relays)) // bit) * length
            region = outs[i].at[target, pl.ds(pl.multiple_of(first, length), length)]
            slot = 3 + 2 * level + k
            copy = remote(
                region, region, send.at[i, slot], recv.at[i, slot], "rep", flip(rep, bit)
            )
            copy.start()
            copies.append(copy)
    for i in range(late, gathered):
        pass_on(i)
    for _, _, _, _, copies in shared:
        copies[-1].wait_recv()
        for copy in copies:
            copy.wait_send()
    for far, near, own, relay in pending:
        far.wait_send()
        near.wait()
        own.wait()
        relay.wait()
    for copy in whole_copies + own_copies:
        copy.wait()


def gather(collective, gathered, swapped, kinds, n_shard, n_rep=1):
    arrays = tuple(gathered) + tuple(swapped)
    shapes = [jax.ShapeDtypeStruct((n_shard,) + a.shape, a.dtype) for a in gathered]
    blocks = [
        jax.ShapeDtypeStruct((n_shard, a.shape[0], a.shape[1] // n_shard), a.dtype)
        for a in swapped
    ]
    relays = 0
    if swapped:
        relays = min(2, n_rep.bit_length() - 1)
        while relays and any(a.shape[0] % (16 << relays) for a in swapped):
            relays -= 1
    return pl.pallas_call(
        functools.partial(gather_kernel, len(gathered), tuple(kinds), relays),
        out_shape=tuple(shapes + blocks),
        in_specs=[VMEM] * len(arrays),
        out_specs=tuple([VMEM] * len(arrays)),
        scratch_shapes=[pltpu.VMEM(b.shape, b.dtype) for b in blocks]
        + [
            pltpu.SemaphoreType.DMA((len(arrays), 3 + 2 * relays)),
            pltpu.SemaphoreType.DMA((len(arrays), 3 + 2 * relays)),
            pltpu.SemaphoreType.DMA((len(arrays),)),
        ],
        compiler_params=pltpu.CompilerParams(collective_id=collective, has_side_effects=True),
    )(*arrays)


def scatter_kernel(total, *refs):
    ins, outs = refs[:total], refs[total : 2 * total]
    near_buf, out_buf, far_buf, send, recv = refs[2 * total :]
    me = lax.axis_index("shard")
    partners = shard_partners(me)[:2]
    greet(partners)
    (_, core), (_, chip) = partners
    diagonal = flip(core, 2)
    first, second, third = [], [], []
    for i in range(total):
        a = remote(
            ins[i].at[diagonal], near_buf.at[i, 0], send.at[i, 0], recv.at[i, 0], "shard", core
        )
        a.start()
        b = remote(ins[i].at[core], near_buf.at[i, 1], send.at[i, 1], recv.at[i, 1], "shard", core)
        b.start()
        first.append(a)
        second.append(b)
    for i in range(total):
        first[i].wait_recv()
        out_buf[i] = (
            ins[i][chip].astype(jnp.float32) + near_buf[i, 0].astype(jnp.float32)
        ).astype(jnp.bfloat16)
        c = remote(out_buf.at[i], far_buf.at[i], send.at[i, 2], recv.at[i, 2], "shard", chip)
        c.start()
        third.append(c)
    for i in range(total):
        second[i].wait_recv()
        outs[i][...] = ins[i][me].astype(jnp.float32) + near_buf[i, 1].astype(jnp.float32)
    for i in range(total):
        third[i].wait_recv()
        outs[i][...] += far_buf[i].astype(jnp.float32)
    for i in range(total):
        first[i].wait_send()
        second[i].wait_send()
        third[i].wait_send()


def scatter(collective, arrays):
    total = len(arrays)
    block = arrays[0].shape[1:]
    return pl.pallas_call(
        functools.partial(scatter_kernel, total),
        out_shape=tuple([jax.ShapeDtypeStruct(block, jnp.float32)] * total),
        in_specs=[VMEM] * total,
        out_specs=tuple([VMEM] * total),
        scratch_shapes=[
            pltpu.VMEM((total, 2) + block, jnp.bfloat16),
            pltpu.VMEM((total,) + block, jnp.bfloat16),
            pltpu.VMEM((total,) + block, jnp.bfloat16),
            pltpu.SemaphoreType.DMA((total, 3)),
            pltpu.SemaphoreType.DMA((total, 3)),
        ],
        compiler_params=pltpu.CompilerParams(collective_id=collective, has_side_effects=True),
    )(*arrays)


def halves(order, me):
    length = 1 << len(order)
    offset = 0
    plan = []
    for bit in order:
        length //= 2
        side = (me // bit) % 2
        plan.append((bit, offset + side * length, offset + (1 - side) * length, length))
        offset = offset + side * length
    return plan


class Stream:
    def __init__(self, buffer, base, rows, order, swap):
        self.buffer, self.base, self.rows, self.order, self.swap = buffer, base, rows, order, swap


def streams_of(buffer, rows, n_rep, swap):
    tiles = -(-rows // (16 * n_rep))
    low_first = tuple(1 << i for i in range(n_rep.bit_length() - 1))
    orders = (low_first, low_first[1::-1] + low_first[2:])
    streams = []
    base = 0
    for share, order in zip((tiles - tiles // 4, tiles // 4), orders):
        if share:
            streams.append(Stream(buffer, base, 16 * share, order, swap))
            base += 16 * share * n_rep
    return streams, base


class RepSum:
    def __init__(self, streams, acc, box, res, sems):
        self.streams, self.acc, self.box, self.res = streams, acc, box, res
        self.send, self.recv, self.swap_send, self.swap_recv, self.local_sem = sems
        self.rep = lax.axis_index("rep")
        self.me = lax.axis_index("shard")
        self.group = shard_partners(self.me)
        self.steps = len(streams[0].order)
        self.plans = [halves(stream.order, self.rep) for stream in streams]
        self.started = [[] for _ in streams]

    def at(self, ref, i, piece, length, lead=None):
        stream = self.streams[i]
        start = stream.base + piece * stream.rows
        if not isinstance(start, int):
            start = pl.multiple_of(start, 16)
        rows = pl.ds(start, length * stream.rows)
        if not stream.swap:
            return ref.at[rows]
        return ref.at[slice(None) if lead is None else lead, rows]

    def begin(self, i, k):
        stream, plan, steps = self.streams[i], self.plans[i], self.steps
        acc, box, res = (refs[stream.buffer] for refs in (self.acc, self.box, self.res))
        if k < steps:
            bit, _, sent, length = plan[k]
            copies = [
                remote(
                    self.at(acc, i, sent, length),
                    self.at(box, i, length, length),
                    self.send.at[i, k],
                    self.recv.at[i, k],
                    "rep",
                    flip(self.rep, bit),
                )
            ]
        elif k == steps:
            mine = plan[-1][1]
            if not stream.swap:
                copies = [
                    pltpu.make_async_copy(
                        self.at(acc, i, mine, 1), self.at(res, i, mine, 1), self.local_sem.at[i]
                    )
                ]
            else:
                target_block = self.at(res, i, mine, 1, self.me)
                copies = [
                    remote(
                        self.at(acc, i, mine, 1, target),
                        target_block,
                        self.swap_send.at[i, j],
                        self.swap_recv.at[i, j],
                        "shard",
                        target,
                    )
                    for j, (_, target) in enumerate(self.group)
                ]
                copies.append(
                    pltpu.make_async_copy(
                        self.at(acc, i, mine, 1, self.me), target_block, self.local_sem.at[i]
                    )
                )
        else:
            bit, kept, _, length = plan[2 * steps - k]
            region = self.at(res, i, kept, length)
            copies = [
                remote(
                    region,
                    region,
                    self.send.at[i, k - 1],
                    self.recv.at[i, k - 1],
                    "rep",
                    flip(self.rep, bit),
                )
            ]
        for copy in copies:
            copy.start()
        self.started[i].append(copies)

    def finish(self, i, k):
        copies, stream = self.started[i][k], self.streams[i]
        if k == self.steps:
            for copy in copies:
                copy.wait()
            return
        copies[0].wait_recv()
        if k > self.steps:
            return
        acc, box = self.acc[stream.buffer], self.box[stream.buffer]
        _, kept, _, length = self.plans[i][k]
        blocks = range(acc.shape[0]) if stream.swap else (None,)

        @pl.loop(0, length)
        def _(p):
            to = pl.multiple_of(stream.base + (kept + p) * stream.rows, 16)
            of = pl.multiple_of(stream.base + (length + p) * stream.rows, 16)
            to, of = pl.ds(to, stream.rows), pl.ds(of, stream.rows)
            for block in blocks:
                x, y = ((to,), (of,)) if block is None else ((block, to), (block, of))
                acc[x] = (acc[x].astype(jnp.float32) + box[y].astype(jnp.float32)).astype(
                    jnp.bfloat16
                )

    def begin_all(self, chosen):
        for i in chosen:
            self.begin(i, 0)

    def step(self, chosen, k):
        for i in chosen:
            self.finish(i, k)
            if k < 2 * self.steps:
                self.begin(i, k + 1)

    def close(self, chosen):
        for i in chosen:
            for k in range(2 * self.steps + 1):
                if k != self.steps:
                    self.started[i][k][0].wait_send()


def pack_columns(source, target, gain):
    blocks, rows, columns = source.shape
    full, rest = divmod(columns, LANES)
    for s in range(blocks):
        for j in range(full):
            target[s, j * rows : (j + 1) * rows] = source[s, :, j * LANES : (j + 1) * LANES]
        at = full * rows
        if rest:
            half = rows // 2
            target[s, at : at + half, :rest] = source[s, :half, full * LANES :]
            target[s, at : at + half, rest:] = source[s, half:, full * LANES :]
            at += half
        target[s, at : at + 16] = gain[s]
        if at + 16 < target.shape[1]:
            target[s, at + 16 :] = jnp.zeros((target.shape[1] - at - 16, LANES), target.dtype)


def unpack_columns(source, out, gain_out, kinds):
    blocks = source.shape[0]
    rows, width = out.shape
    columns = width // blocks
    size = columns // kinds
    full, rest = divmod(columns, LANES)
    half = rows // 2
    at = full * rows
    gain = jnp.zeros((16, LANES), jnp.float32)
    for t in range(blocks):
        parts = [source[t, j * rows : (j + 1) * rows] for j in range(full)]
        end = at
        if rest:
            tail = source[t, at : at + half]
            parts.append(jnp.concatenate([tail[:, :rest], tail[:, rest:]], axis=0))
            end += half
        block = jnp.concatenate(parts, axis=1)
        gain += source[t, end : end + 16].astype(jnp.float32)
        for kind in range(kinds):
            start = (kind * blocks + t) * size
            out[:, start : start + size] = block[:, kind * size : (kind + 1) * size]
    gain_out[...] = gain


def pack_rows(sources, target):
    tall = sum(source.shape[0] for source in sources)
    at = 0
    for source in sources:
        rows = source.shape[0]
        for j in range(source.shape[1] // LANES):
            target[j * tall + at : j * tall + at + rows] = source[:, j * LANES : (j + 1) * LANES]
        at += rows
    end = tall * sources[0].shape[1] // LANES
    if end < target.shape[0]:
        target[end:] = jnp.zeros((target.shape[0] - end, LANES), target.dtype)


def unpack_rows(source, outs):
    tall = sum(out.shape[0] for out in outs)
    at = 0
    for out in outs:
        rows = out.shape[0]
        for j in range(out.shape[1] // LANES):
            out[:, j * LANES : (j + 1) * LANES] = source[
                j * tall + at : j * tall + at + rows
            ]
        at += rows


def column_rows(shape):
    _, rows, columns = shape
    return rows * columns // LANES + 16


def sum_kernel(streams, qkv, gain1, win, gain2, gout, gdown, *refs):
    o_qkv, o_gain1, o_in, o_gain2, o_out, o_down = refs[:6]
    acc, box, res = refs[6:9], refs[9:12], refs[12:15]
    pack_rows((gout, gdown), acc[0])
    pack_columns(win, acc[1], gain2)
    pack_columns(qkv, acc[2], gain1)
    rep_sum = RepSum(streams, acc, box, res, refs[15:])
    bits = sorted(streams[0].order)
    greet([("rep", flip(rep_sum.rep, bit)) for bit in bits] + rep_sum.group)
    chosen = range(len(streams))
    rep_sum.begin_all(chosen)
    for k in range(2 * rep_sum.steps + 1):
        rep_sum.step(chosen, k)
    unpack_rows(res[0], (o_out, o_down))
    unpack_columns(res[1], o_in, o_gain2, 2)
    unpack_columns(res[2], o_qkv, o_gain1, 3)
    rep_sum.close(chosen)


def sum_over_rep(collective, n_rep, qkv, gain1, win, gain2, gout, gdown):
    b16, f32 = jnp.bfloat16, jnp.float32
    n_shard, part, columns = qkv.shape
    width = columns * n_shard
    plain_rows = (gout.shape[0] + gdown.shape[0]) * gout.shape[1] // LANES
    streams, shapes = [], []
    for i, (rows, swap) in enumerate(
        ((plain_rows, False), (column_rows(win.shape), True), (column_rows(qkv.shape), True))
    ):
        more, padded = streams_of(i, rows, n_rep, swap)
        streams += more
        shapes.append((n_shard, padded, LANES) if swap else (padded, LANES))
    steps = len(streams[0].order)
    count = len(streams)
    outs = [(part, width), (16, LANES), (part, win.shape[2] * n_shard), (16, LANES)]
    outs += [gout.shape, gdown.shape]
    return pl.pallas_call(
        functools.partial(sum_kernel, streams),
        out_shape=tuple(
            jax.ShapeDtypeStruct(shape, f32 if shape == (16, LANES) else b16) for shape in outs
        ),
        in_specs=[VMEM] * 6,
        out_specs=tuple([VMEM] * 6),
        scratch_shapes=[pltpu.VMEM(shape, b16) for shape in shapes * 3]
        + [
            pltpu.SemaphoreType.DMA((count, 2 * steps)),
            pltpu.SemaphoreType.DMA((count, 2 * steps)),
            pltpu.SemaphoreType.DMA((count, 3)),
            pltpu.SemaphoreType.DMA((count, 3)),
            pltpu.SemaphoreType.DMA((count,)),
        ],
        compiler_params=pltpu.CompilerParams(collective_id=collective, has_side_effects=True),
    )(qkv, gain1, win, gain2, gout, gdown)


def local(
    n_shard, n_rep, tokens, gain_one, qkv_weight, out_weight, gain_two, in_weight, down_weight,
    grad_output
):
    tok_dev, width = tokens.shape[1:]
    part = width // n_shard
    heads = part // HEAD_DIM
    hidden = down_weight.shape[0]
    count = tok_dev * n_shard
    scale = HEAD_DIM ** (-0.5)
    f32, b16 = jnp.float32, jnp.bfloat16
    own_tokens = tokens.reshape(tok_dev, width)
    own_grad = grad_output.reshape(tok_dev, width)

    all_tokens, all_g1, all_g2, all_grad, my_qkv, my_in = gather(
        0,
        (own_tokens, gain_one.reshape(1, part), gain_two.reshape(1, part), own_grad),
        (qkv_weight, in_weight),
        (3, 2),
        n_shard,
        n_rep,
    )
    full_g1 = all_g1.reshape(width)
    full_g2 = all_g2.reshape(width)
    my_qkv = my_qkv.reshape(width, 3 * part)
    my_in = my_in.reshape(width, 2 * hidden)
    grad_b = all_grad.reshape(count, width)

    inputs = own_tokens.astype(f32)
    normed_one, inverse_one, _ = layer_norm(inputs, full_g1)
    hidden_one = layer_norm(all_tokens.reshape(count, width).astype(f32), full_g1)[2].astype(b16)
    projected = jnp.dot(hidden_one, my_qkv, preferred_element_type=f32)
    cosine, sine = rotary_tables(count, HEAD_DIM)
    split = projected.reshape(count, 3, heads, HEAD_DIM).transpose(1, 2, 0, 3)
    queries, key_raw = split[0], split[1]
    query_rot = (queries * cosine + rotate_half(queries) * sine).astype(b16)
    key_rot = (key_raw * cosine + rotate_half(key_raw) * sine).astype(b16)
    values = split[2].astype(b16)
    scores = jnp.einsum("hqd,hkd->hqk", query_rot, key_rot, preferred_element_type=f32) * scale
    maxima = jnp.max(scores, axis=-1, keepdims=True)
    expo = jnp.exp(scores - maxima)
    totals = jnp.sum(expo, axis=-1, keepdims=True)
    accum = jnp.einsum("hqk,hkd->hqd", expo.astype(b16), values, preferred_element_type=f32)
    att_heads = (accum / totals).astype(b16)
    attended = att_heads.transpose(1, 0, 2).reshape(count, part)
    partial = jnp.dot(attended, out_weight, preferred_element_type=f32).astype(b16)
    (mixed,) = scatter(1, (partial.reshape(n_shard, tok_dev, width),))
    resid = inputs + mixed
    normed_two, inverse_two, scaled_two = layer_norm(resid, full_g2)
    (hidden_two,) = gather(2, (scaled_two.astype(b16),), (), (), n_shard)
    hidden_two = hidden_two.reshape(count, width)
    upper = jnp.dot(hidden_two, my_in, preferred_element_type=f32)
    inner, gate_half = upper[:, :hidden], upper[:, hidden:]
    gelu_value, gelu_slope = gelu_pair(inner)
    act = (gelu_value * gate_half).astype(b16)
    down_part = jnp.dot(act, down_weight, preferred_element_type=f32).astype(b16)
    grad_down = outer_sum(act, grad_b)
    grad_act = times_transposed(grad_b, down_weight)
    grad_upper = jnp.concatenate(
        [grad_act * gate_half * gelu_slope, grad_act * gelu_value], axis=-1
    ).astype(b16)
    grad_in = outer_sum(hidden_two, grad_upper)
    h2_part = times_transposed(grad_upper, my_in).astype(b16)
    down_sum, grad_h2 = scatter(
        3, (down_part.reshape(n_shard, tok_dev, width), h2_part.reshape(n_shard, tok_dev, width))
    )
    output = (resid + down_sum).astype(b16)
    norm_grad_two, grad_gain_two = norm_backward(grad_h2, normed_two, inverse_two, full_g2)
    grad_resid = own_grad.astype(f32) + norm_grad_two
    (resid_b,) = gather(4, (grad_resid.astype(b16),), (), (), n_shard)
    resid_b = resid_b.reshape(count, width)
    grad_out = outer_sum(attended, resid_b)
    grad_att = times_transposed(resid_b, out_weight).astype(b16)
    grad_heads = grad_att.reshape(count, heads, HEAD_DIM).transpose(1, 0, 2)
    delta = jnp.sum(grad_heads.astype(f32) * att_heads.astype(f32), axis=-1, keepdims=True)
    probs = expo / totals
    grad_value = jnp.einsum(
        "hqk,hqd->khd", probs.astype(b16), grad_heads, preferred_element_type=f32
    )
    grad_probs = jnp.einsum("hqd,hkd->hqk", grad_heads, values, preferred_element_type=f32)
    grad_scores = (probs * (grad_probs - delta) * scale).astype(b16)
    grad_qr = jnp.einsum("hqk,hkd->hqd", grad_scores, key_rot, preferred_element_type=f32)
    grad_kr = jnp.einsum("hqk,hqd->hkd", grad_scores, query_rot, preferred_element_type=f32)
    grad_q = (grad_qr * cosine - rotate_half(grad_qr) * sine).transpose(1, 0, 2)
    grad_k = (grad_kr * cosine - rotate_half(grad_kr) * sine).transpose(1, 0, 2)
    grad_projected = jnp.concatenate(
        [g.reshape(count, part) for g in (grad_q, grad_k, grad_value)], axis=-1
    ).astype(b16)
    grad_qkv = outer_sum(hidden_one, grad_projected)
    h1_part = times_transposed(grad_projected, my_qkv).astype(b16)
    (grad_h1,) = scatter(5, (h1_part.reshape(n_shard, tok_dev, width),))
    norm_grad_one, grad_gain_one = norm_backward(grad_h1, normed_one, inverse_one, full_g1)
    grad_tokens = grad_resid + norm_grad_one

    def gain_rows(gain):
        room = -part % LANES
        rows = jnp.pad(gain.reshape(n_shard, part), ((0, 0), (0, room)))
        rows = rows.reshape(n_shard, -1, LANES)
        return jnp.pad(rows, ((0, 0), (0, 16 - rows.shape[1]), (0, 0))).astype(b16)

    sum_qkv, sum_g1, sum_in, sum_g2, sum_out, sum_down = sum_over_rep(
        6,
        n_rep,
        grad_qkv.astype(b16).reshape(n_shard, part, -1),
        gain_rows(grad_gain_one),
        grad_in.astype(b16).reshape(n_shard, part, -1),
        gain_rows(grad_gain_two),
        grad_out.astype(b16),
        grad_down.astype(b16),
    )
    return (
        output.reshape(1, tok_dev, width),
        grad_tokens.reshape(1, tok_dev, width),
        sum_g1.reshape(-1)[:part],
        sum_qkv.astype(f32),
        sum_out.astype(f32),
        sum_g2.reshape(-1)[:part],
        sum_in.astype(f32),
        sum_down.astype(f32),
    )


def solution(mesh):
    in_specs = (
        P("rep", "shard", None),
        P("shard"),
        P("shard", None),
        P("shard", None),
        P("shard"),
        P("shard", None),
        P("shard", None),
        P("rep", "shard", None),
    )
    out_specs = (
        P("rep", "shard", None),
        P("rep", "shard", None),
        P("shard"),
        P("shard", None),
        P("shard", None),
        P("shard"),
        P("shard", None),
        P("shard", None),
    )
    body = functools.partial(local, mesh.shape["shard"], mesh.shape["rep"])
    return jax.shard_map(body, mesh=mesh, in_specs=in_specs, out_specs=out_specs, check_vma=False)
```

```python
import functools

import jax
import jax.numpy as jnp
from jax import lax
from jax.experimental import pallas as pl
from jax.experimental.pallas import tpu as pltpu
from jax.sharding import PartitionSpec as P

HEAD_DIM = 64
EPSILON = 1e-05
THETA = 160000.0
SQRT_HALF = 0.7071067811865476
INV_SQRT_TAU = 0.3989422804014327
MESH_ID = pl.DeviceIdType.MESH
LANES = 128
VMEM = pl.BlockSpec(memory_space=pltpu.VMEM)


def layer_norm(values, gain):
    mean_row = jnp.mean(values, axis=-1, keepdims=True)
    centred = values - mean_row
    variance = jnp.mean(centred * centred, axis=-1, keepdims=True)
    inverse = lax.rsqrt(variance + EPSILON)
    normed = centred * inverse
    return (normed, inverse, normed * gain.astype(jnp.float32))


def norm_backward(grad_out, normed, inverse, gain):
    grad_normed = grad_out * gain.astype(jnp.float32)
    gain_grad = jnp.sum(grad_out * normed, axis=0)
    first = jnp.mean(grad_normed, axis=-1, keepdims=True)
    second = jnp.mean(grad_normed * normed, axis=-1, keepdims=True)
    return (inverse * (grad_normed - first - normed * second), gain_grad)


def rotary_tables(count, head_dim):
    half = head_dim // 2
    positions = jnp.arange(count, dtype=jnp.int32)
    freq = THETA ** (-jnp.arange(half, dtype=jnp.float32) * 2.0 / head_dim)
    angles = positions.astype(jnp.float32)[:, None] * freq[None, :]
    angles = jnp.concatenate([angles, angles], axis=-1)
    return (jnp.cos(angles)[None], jnp.sin(angles)[None])


def rotate_half(values):
    half = values.shape[-1] // 2
    return jnp.concatenate([-values[..., half:], values[..., :half]], axis=-1)


def gelu_pair(inner):
    cdf = 0.5 * (1.0 + jax.scipy.special.erf(inner * SQRT_HALF))
    return (inner * cdf, cdf + inner * jnp.exp(-0.5 * inner * inner) * INV_SQRT_TAU)


def outer_sum(left, right):
    return lax.dot_general(
        left, right, (((0,), (0,)), ((), ())), preferred_element_type=jnp.float32
    )


def times_transposed(left, weight):
    return lax.dot_general(
        left, weight, (((1,), (1,)), ((), ())), preferred_element_type=jnp.float32
    )


def flip(index, bit):
    return index + bit * (1 - 2 * ((index // bit) % 2))


def remote(src, dst, send, recv, axis, target):
    return pltpu.make_async_remote_copy(
        src_ref=src,
        dst_ref=dst,
        send_sem=send,
        recv_sem=recv,
        device_id={axis: target},
        device_id_type=MESH_ID,
    )


def greet(partners):
    barrier = pltpu.get_barrier_semaphore()
    for axis, target in partners:
        pl.semaphore_signal(barrier, inc=1, device_id={axis: target}, device_id_type=MESH_ID)
    pl.semaphore_wait(barrier, len(partners))


def shard_partners(me):
    return [("shard", flip(me, 1)), ("shard", flip(me, 2)), ("shard", flip(flip(me, 1), 2))]


def gather_kernel(gathered, kinds, relays, *refs):
    total = gathered + len(kinds)
    ins, outs = refs[:total], refs[total : 2 * total]
    packed = refs[2 * total : 2 * total + len(kinds)]
    send, recv, local_sem = refs[2 * total + len(kinds) :]
    me = lax.axis_index("shard")
    partners = shard_partners(me)
    rep = lax.axis_index("rep")
    bits = [1 << b for b in range(relays)] if kinds else []
    greet(partners + [("rep", flip(rep, bit)) for bit in bits])
    (_, core), (_, chip), (_, diagonal) = partners
    pending = []

    def begin(i):
        far = remote(ins[i], outs[i].at[me], send.at[i, 0], recv.at[i, 0], "shard", chip)
        far.start()
        near = remote(ins[i], outs[i].at[me], send.at[i, 1], recv.at[i, 1], "shard", core)
        near.start()
        own = pltpu.make_async_copy(ins[i], outs[i].at[me], local_sem.at[i])
        own.start()
        pending.append((far, near, own))

    def pass_on(i):
        pending[i][0].wait_recv()
        relay = remote(
            outs[i].at[chip], outs[i].at[chip], send.at[i, 2], recv.at[i, 2], "shard", core
        )
        relay.start()
        pending[i] = pending[i] + (relay,)

    late = gathered - 1 if kinds else gathered
    for i in range(late):
        begin(i)
    shared, whole_copies, own_copies = [], [], []
    for i in range(gathered, total):
        source, buffer, kind_count = ins[i], packed[i - gathered], kinds[i - gathered]
        blocks, tall, columns = buffer.shape
        size = columns // kind_count
        for j in range(blocks):
            for kind in range(kind_count):
                start = (kind * blocks + j) * size
                buffer[j, :, kind * size : (kind + 1) * size] = source[:, start : start + size]
        share = tall >> relays
        rows = pl.ds(pl.multiple_of((rep % (1 << relays)) * share, share), share)
        for k, target in enumerate((chip, diagonal)):
            copy = remote(
                buffer.at[target, rows],
                outs[i].at[me, rows],
                send.at[i, k],
                recv.at[i, k],
                "shard",
                target,
            )
            copy.start()
            shared.append((i, k, target, tall, [copy]))
        copy = remote(
            buffer.at[core], outs[i].at[me], send.at[i, 2], recv.at[i, 2], "shard", core
        )
        copy.start()
        whole_copies.append(copy)
        own = pltpu.make_async_copy(buffer.at[me], outs[i].at[me], local_sem.at[i])
        own.start()
        own_copies.append(own)
    for i in range(late, gathered):
        begin(i)
    for i in range(late):
        pass_on(i)
    for level, bit in enumerate(bits):
        for i, k, target, tall, copies in shared:
            copies[-1].wait_recv()
            length = (tall >> relays) * bit
            first = ((rep % (1 << relays)) // bit) * length
            region = outs[i].at[target, pl.ds(pl.multiple_of(first, length), length)]
            slot = 3 + 2 * level + k
            copy = remote(
                region, region, send.at[i, slot], recv.at[i, slot], "rep", flip(rep, bit)
            )
            copy.start()
            copies.append(copy)
    for i in range(late, gathered):
        pass_on(i)
    for _, _, _, _, copies in shared:
        copies[-1].wait_recv()
        for copy in copies:
            copy.wait_send()
    for far, near, own, relay in pending:
        far.wait_send()
        near.wait()
        own.wait()
        relay.wait()
    for copy in whole_copies + own_copies:
        copy.wait()


def gather(collective, gathered, swapped, kinds, n_shard, n_rep=1):
    arrays = tuple(gathered) + tuple(swapped)
    shapes = [jax.ShapeDtypeStruct((n_shard,) + a.shape, a.dtype) for a in gathered]
    blocks = [
        jax.ShapeDtypeStruct((n_shard, a.shape[0], a.shape[1] // n_shard), a.dtype)
        for a in swapped
    ]
    relays = 0
    if swapped:
        relays = min(2, n_rep.bit_length() - 1)
        while relays and any(a.shape[0] % (16 << relays) for a in swapped):
            relays -= 1
    return pl.pallas_call(
        functools.partial(gather_kernel, len(gathered), tuple(kinds), relays),
        out_shape=tuple(shapes + blocks),
        in_specs=[VMEM] * len(arrays),
        out_specs=tuple([VMEM] * len(arrays)),
        scratch_shapes=[pltpu.VMEM(b.shape, b.dtype) for b in blocks]
        + [
            pltpu.SemaphoreType.DMA((len(arrays), 3 + 2 * relays)),
            pltpu.SemaphoreType.DMA((len(arrays), 3 + 2 * relays)),
            pltpu.SemaphoreType.DMA((len(arrays),)),
        ],
        compiler_params=pltpu.CompilerParams(collective_id=collective, has_side_effects=True),
    )(*arrays)


def scatter_kernel(total, *refs):
    ins, outs = refs[:total], refs[total : 2 * total]
    near_buf, out_buf, far_buf, send, recv = refs[2 * total :]
    me = lax.axis_index("shard")
    partners = shard_partners(me)[:2]
    greet(partners)
    (_, core), (_, chip) = partners
    diagonal = flip(core, 2)
    first, second, third = [], [], []
    for i in range(total):
        a = remote(
            ins[i].at[diagonal], near_buf.at[i, 0], send.at[i, 0], recv.at[i, 0], "shard", core
        )
        a.start()
        b = remote(ins[i].at[core], near_buf.at[i, 1], send.at[i, 1], recv.at[i, 1], "shard", core)
        b.start()
        first.append(a)
        second.append(b)
    for i in range(total):
        first[i].wait_recv()
        out_buf[i] = (
            ins[i][chip].astype(jnp.float32) + near_buf[i, 0].astype(jnp.float32)
        ).astype(jnp.bfloat16)
        c = remote(out_buf.at[i], far_buf.at[i], send.at[i, 2], recv.at[i, 2], "shard", chip)
        c.start()
        third.append(c)
    for i in range(total):
        second[i].wait_recv()
        outs[i][...] = ins[i][me].astype(jnp.float32) + near_buf[i, 1].astype(jnp.float32)
    for i in range(total):
        third[i].wait_recv()
        outs[i][...] += far_buf[i].astype(jnp.float32)
    for i in range(total):
        first[i].wait_send()
        second[i].wait_send()
        third[i].wait_send()


def scatter(collective, arrays):
    total = len(arrays)
    block = arrays[0].shape[1:]
    return pl.pallas_call(
        functools.partial(scatter_kernel, total),
        out_shape=tuple([jax.ShapeDtypeStruct(block, jnp.float32)] * total),
        in_specs=[VMEM] * total,
        out_specs=tuple([VMEM] * total),
        scratch_shapes=[
            pltpu.VMEM((total, 2) + block, jnp.bfloat16),
            pltpu.VMEM((total,) + block, jnp.bfloat16),
            pltpu.VMEM((total,) + block, jnp.bfloat16),
            pltpu.SemaphoreType.DMA((total, 3)),
            pltpu.SemaphoreType.DMA((total, 3)),
        ],
        compiler_params=pltpu.CompilerParams(collective_id=collective, has_side_effects=True),
    )(*arrays)


def halves(order, me):
    length = 1 << len(order)
    offset = 0
    plan = []
    for bit in order:
        length //= 2
        side = (me // bit) % 2
        plan.append((bit, offset + side * length, offset + (1 - side) * length, length))
        offset = offset + side * length
    return plan


class Stream:
    def __init__(self, buffer, base, rows, order, swap):
        self.buffer, self.base, self.rows, self.order, self.swap = buffer, base, rows, order, swap


def streams_of(buffer, rows, n_rep, swap):
    tiles = -(-rows // (16 * n_rep))
    low_first = tuple(1 << i for i in range(n_rep.bit_length() - 1))
    orders = (low_first, low_first[1::-1] + low_first[2:])
    streams = []
    base = 0
    for share, order in zip((tiles - tiles // 2, tiles // 2), orders):
        if share:
            streams.append(Stream(buffer, base, 16 * share, order, swap))
            base += 16 * share * n_rep
    return streams, base


class RepSum:
    def __init__(self, streams, acc, box, res, sems):
        self.streams, self.acc, self.box, self.res = streams, acc, box, res
        self.send, self.recv, self.swap_send, self.swap_recv, self.local_sem = sems
        self.rep = lax.axis_index("rep")
        self.me = lax.axis_index("shard")
        self.group = shard_partners(self.me)
        self.steps = len(streams[0].order)
        self.plans = [halves(stream.order, self.rep) for stream in streams]
        self.started = [[] for _ in streams]

    def at(self, ref, i, piece, length, lead=None):
        stream = self.streams[i]
        start = stream.base + piece * stream.rows
        if not isinstance(start, int):
            start = pl.multiple_of(start, 16)
        rows = pl.ds(start, length * stream.rows)
        if not stream.swap:
            return ref.at[rows]
        return ref.at[slice(None) if lead is None else lead, rows]

    def begin(self, i, k):
        stream, plan, steps = self.streams[i], self.plans[i], self.steps
        acc, box, res = (refs[stream.buffer] for refs in (self.acc, self.box, self.res))
        if k < steps:
            bit, _, sent, length = plan[k]
            copies = [
                remote(
                    self.at(acc, i, sent, length),
                    self.at(box, i, length, length),
                    self.send.at[i, k],
                    self.recv.at[i, k],
                    "rep",
                    flip(self.rep, bit),
                )
            ]
        elif k == steps:
            mine = plan[-1][1]
            if not stream.swap:
                copies = [
                    pltpu.make_async_copy(
                        self.at(acc, i, mine, 1), self.at(res, i, mine, 1), self.local_sem.at[i]
                    )
                ]
            else:
                target_block = self.at(res, i, mine, 1, self.me)
                copies = [
                    remote(
                        self.at(acc, i, mine, 1, target),
                        target_block,
                        self.swap_send.at[i, j],
                        self.swap_recv.at[i, j],
                        "shard",
                        target,
                    )
                    for j, (_, target) in enumerate(self.group)
                ]
                copies.append(
                    pltpu.make_async_copy(
                        self.at(acc, i, mine, 1, self.me), target_block, self.local_sem.at[i]
                    )
                )
        else:
            bit, kept, _, length = plan[2 * steps - k]
            region = self.at(res, i, kept, length)
            copies = [
                remote(
                    region,
                    region,
                    self.send.at[i, k - 1],
                    self.recv.at[i, k - 1],
                    "rep",
                    flip(self.rep, bit),
                )
            ]
        for copy in copies:
            copy.start()
        self.started[i].append(copies)

    def finish(self, i, k):
        copies, stream = self.started[i][k], self.streams[i]
        if k == self.steps:
            for copy in copies:
                copy.wait()
            return
        copies[0].wait_recv()
        if k > self.steps:
            return
        acc, box = self.acc[stream.buffer], self.box[stream.buffer]
        _, kept, _, length = self.plans[i][k]
        blocks = range(acc.shape[0]) if stream.swap else (None,)

        @pl.loop(0, length)
        def _(p):
            to = pl.multiple_of(stream.base + (kept + p) * stream.rows, 16)
            of = pl.multiple_of(stream.base + (length + p) * stream.rows, 16)
            to, of = pl.ds(to, stream.rows), pl.ds(of, stream.rows)
            for block in blocks:
                x, y = ((to,), (of,)) if block is None else ((block, to), (block, of))
                acc[x] = (acc[x].astype(jnp.float32) + box[y].astype(jnp.float32)).astype(
                    jnp.bfloat16
                )

    def begin_all(self, chosen):
        for i in chosen:
            self.begin(i, 0)

    def step(self, i, k):
        self.finish(i, k)
        if k < 2 * self.steps:
            self.begin(i, k + 1)

    def close(self, chosen):
        for i in chosen:
            for k in range(2 * self.steps + 1):
                if k != self.steps:
                    self.started[i][k][0].wait_send()


def pack_columns(source, target, gain):
    blocks, rows, columns = source.shape
    full, rest = divmod(columns, LANES)
    for s in range(blocks):
        for j in range(full):
            target[s, j * rows : (j + 1) * rows] = source[s, :, j * LANES : (j + 1) * LANES]
        at = full * rows
        if rest:
            half = rows // 2
            target[s, at : at + half, :rest] = source[s, :half, full * LANES :]
            target[s, at : at + half, rest:] = source[s, half:, full * LANES :]
            at += half
        if gain is not None:
            target[s, at : at + 16] = gain[s]
            at += 16
        if at < target.shape[1]:
            target[s, at:] = jnp.zeros((target.shape[1] - at, LANES), target.dtype)


def pack_gain(gain, target, at):
    blocks = target.shape[0]
    part = gain.shape[1] // blocks
    row = lax.broadcasted_iota(jnp.int32, (16, LANES), 0)
    for s in range(blocks):
        tile = jnp.zeros((16, LANES), jnp.float32)
        for j in range(-(-part // LANES)):
            piece = gain[:, s * part + j * LANES : s * part + min((j + 1) * LANES, part)]
            room = LANES - piece.shape[1]
            if room:
                piece = jnp.concatenate([piece, jnp.zeros((1, room), jnp.float32)], axis=1)
            tile = jnp.where(row == j, jnp.broadcast_to(piece, (16, LANES)), tile)
        target[s, at : at + 16] = tile.astype(target.dtype)


def unpack_columns(source, out, gain_out, kinds):
    blocks = source.shape[0]
    rows, width = out.shape
    columns = width // blocks
    size = columns // kinds
    full, rest = divmod(columns, LANES)
    half = rows // 2
    at = full * rows
    gain = jnp.zeros((16, LANES), jnp.float32)
    for t in range(blocks):
        parts = [source[t, j * rows : (j + 1) * rows] for j in range(full)]
        end = at
        if rest:
            tail = source[t, at : at + half]
            parts.append(jnp.concatenate([tail[:, :rest], tail[:, rest:]], axis=0))
            end += half
        block = jnp.concatenate(parts, axis=1)
        gain += source[t, end : end + 16].astype(jnp.float32)
        for kind in range(kinds):
            start = (kind * blocks + t) * size
            out[:, start : start + size] = block[:, kind * size : (kind + 1) * size]
    gain_out[...] = gain


def pack_rows(sources, target):
    tall = sum(source.shape[0] for source in sources)
    at = 0
    for source in sources:
        rows = source.shape[0]
        for j in range(source.shape[1] // LANES):
            target[j * tall + at : j * tall + at + rows] = source[:, j * LANES : (j + 1) * LANES]
        at += rows
    end = tall * sources[0].shape[1] // LANES
    if end < target.shape[0]:
        target[end:] = jnp.zeros((target.shape[0] - end, LANES), target.dtype)


def unpack_rows(source, outs):
    tall = sum(out.shape[0] for out in outs)
    at = 0
    for out in outs:
        rows = out.shape[0]
        for j in range(out.shape[1] // LANES):
            out[:, j * LANES : (j + 1) * LANES] = source[
                j * tall + at : j * tall + at + rows
            ]
        at += rows


def column_rows(shape):
    _, rows, columns = shape
    return rows * columns // LANES + 16


def sum_kernel(streams, early, qkv, h1_part, normed, win, gain2, gout, gdown, *refs):
    o_qkv, o_gain1, o_in, o_gain2, o_out, o_down, o_h1 = refs[:7]
    acc, box, res = refs[7:10], refs[10:13], refs[13:16]
    near_buf, out_buf, far_buf, h1_send, h1_recv = refs[16:21]
    rep_sum = RepSum(streams, acc, box, res, refs[21:])
    me = rep_sum.me
    core, chip = flip(me, 1), flip(me, 2)
    bits = sorted(streams[0].order)
    greet([("rep", flip(rep_sum.rep, bit)) for bit in bits] + rep_sum.group)
    first = [
        remote(
            h1_part.at[target], near_buf.at[j], h1_send.at[j], h1_recv.at[j], "shard", core
        )
        for j, target in enumerate((flip(core, 2), core))
    ]
    for copy in first:
        copy.start()
    pack_rows((gout, gdown), acc[0])
    pack_columns(win, acc[1], gain2)
    rep_sum.begin_all(range(early))
    first[0].wait_recv()
    out_buf[...] = (
        h1_part[chip].astype(jnp.float32) + near_buf[0].astype(jnp.float32)
    ).astype(jnp.bfloat16)
    last = remote(out_buf, far_buf, h1_send.at[2], h1_recv.at[2], "shard", chip)
    last.start()
    pack_columns(qkv, acc[2], None)
    first[1].wait_recv()
    own = h1_part[me].astype(jnp.float32) + near_buf[1].astype(jnp.float32)
    last.wait_recv()
    grad_h1 = own + far_buf[...].astype(jnp.float32)
    o_h1[...] = grad_h1
    gain = jnp.sum(grad_h1 * normed[...], axis=0, keepdims=True)
    pack_gain(gain, acc[2], column_rows(qkv.shape) - 16)
    rep_sum.begin_all(range(early, len(streams)))
    pairs = len(streams) // 2
    for t in range(2 * rep_sum.steps + 1 + pairs):
        for i in range(len(streams)):
            k = t - i // 2
            if 0 <= k <= 2 * rep_sum.steps:
                rep_sum.step(i, k)
    for copy in first + [last]:
        copy.wait_send()
    unpack_rows(res[0], (o_out, o_down))
    unpack_columns(res[1], o_in, o_gain2, 2)
    unpack_columns(res[2], o_qkv, o_gain1, 3)
    rep_sum.close(range(len(streams)))


def sum_over_rep(collective, n_rep, qkv, h1_part, normed, win, gain2, gout, gdown):
    b16, f32 = jnp.bfloat16, jnp.float32
    n_shard, part, columns = qkv.shape
    width = columns * n_shard
    plain_rows = (gout.shape[0] + gdown.shape[0]) * gout.shape[1] // LANES
    streams, shapes, early = [], [], 0
    for i, (rows, swap) in enumerate(
        ((plain_rows, False), (column_rows(win.shape), True), (column_rows(qkv.shape), True))
    ):
        more, padded = streams_of(i, rows, n_rep, swap)
        early = len(streams)
        streams += more
        shapes.append((n_shard, padded, LANES) if swap else (padded, LANES))
    steps = len(streams[0].order)
    count = len(streams)
    outs = [(part, width), (16, LANES), (part, win.shape[2] * n_shard), (16, LANES)]
    outs += [gout.shape, gdown.shape, normed.shape]
    wide = ((16, LANES), normed.shape)
    return pl.pallas_call(
        functools.partial(sum_kernel, streams, early),
        out_shape=tuple(
            jax.ShapeDtypeStruct(shape, f32 if shape in wide else b16) for shape in outs
        ),
        in_specs=[VMEM] * 7,
        out_specs=tuple([VMEM] * 7),
        scratch_shapes=[pltpu.VMEM(shape, b16) for shape in shapes * 3]
        + [
            pltpu.VMEM((2,) + normed.shape, b16),
            pltpu.VMEM(normed.shape, b16),
            pltpu.VMEM(normed.shape, b16),
            pltpu.SemaphoreType.DMA((3,)),
            pltpu.SemaphoreType.DMA((3,)),
            pltpu.SemaphoreType.DMA((count, 2 * steps)),
            pltpu.SemaphoreType.DMA((count, 2 * steps)),
            pltpu.SemaphoreType.DMA((count, 3)),
            pltpu.SemaphoreType.DMA((count, 3)),
            pltpu.SemaphoreType.DMA((count,)),
        ],
        compiler_params=pltpu.CompilerParams(collective_id=collective, has_side_effects=True),
    )(qkv, h1_part, normed, win, gain2, gout, gdown)


def local(
    n_shard, n_rep, tokens, gain_one, qkv_weight, out_weight, gain_two, in_weight, down_weight,
    grad_output
):
    tok_dev, width = tokens.shape[1:]
    part = width // n_shard
    heads = part // HEAD_DIM
    hidden = down_weight.shape[0]
    count = tok_dev * n_shard
    scale = HEAD_DIM ** (-0.5)
    f32, b16 = jnp.float32, jnp.bfloat16
    own_tokens = tokens.reshape(tok_dev, width)
    own_grad = grad_output.reshape(tok_dev, width)

    all_tokens, all_g1, all_g2, all_grad, my_qkv, my_in = gather(
        0,
        (own_tokens, gain_one.reshape(1, part), gain_two.reshape(1, part), own_grad),
        (qkv_weight, in_weight),
        (3, 2),
        n_shard,
        n_rep,
    )
    full_g1 = all_g1.reshape(width)
    full_g2 = all_g2.reshape(width)
    my_qkv = my_qkv.reshape(width, 3 * part)
    my_in = my_in.reshape(width, 2 * hidden)
    grad_b = all_grad.reshape(count, width)

    inputs = own_tokens.astype(f32)
    normed_one, inverse_one, _ = layer_norm(inputs, full_g1)
    hidden_one = layer_norm(all_tokens.reshape(count, width).astype(f32), full_g1)[2].astype(b16)
    projected = jnp.dot(hidden_one, my_qkv, preferred_element_type=f32)
    cosine, sine = rotary_tables(count, HEAD_DIM)
    split = projected.reshape(count, 3, heads, HEAD_DIM).transpose(1, 2, 0, 3)
    queries, key_raw = split[0], split[1]
    query_rot = (queries * cosine + rotate_half(queries) * sine).astype(b16)
    key_rot = (key_raw * cosine + rotate_half(key_raw) * sine).astype(b16)
    values = split[2].astype(b16)
    scores = jnp.einsum("hqd,hkd->hqk", query_rot, key_rot, preferred_element_type=f32) * scale
    maxima = jnp.max(scores, axis=-1, keepdims=True)
    expo = jnp.exp(scores - maxima)
    totals = jnp.sum(expo, axis=-1, keepdims=True)
    accum = jnp.einsum("hqk,hkd->hqd", expo.astype(b16), values, preferred_element_type=f32)
    att_heads = (accum / totals).astype(b16)
    attended = att_heads.transpose(1, 0, 2).reshape(count, part)
    partial = jnp.dot(attended, out_weight, preferred_element_type=f32).astype(b16)
    (mixed,) = scatter(1, (partial.reshape(n_shard, tok_dev, width),))
    resid = inputs + mixed
    normed_two, inverse_two, scaled_two = layer_norm(resid, full_g2)
    (hidden_two,) = gather(2, (scaled_two.astype(b16),), (), (), n_shard)
    hidden_two = hidden_two.reshape(count, width)
    upper = jnp.dot(hidden_two, my_in, preferred_element_type=f32)
    inner, gate_half = upper[:, :hidden], upper[:, hidden:]
    gelu_value, gelu_slope = gelu_pair(inner)
    act = (gelu_value * gate_half).astype(b16)
    down_part = jnp.dot(act, down_weight, preferred_element_type=f32).astype(b16)
    grad_down = outer_sum(act, grad_b)
    grad_act = times_transposed(grad_b, down_weight)
    grad_upper = jnp.concatenate(
        [grad_act * gate_half * gelu_slope, grad_act * gelu_value], axis=-1
    ).astype(b16)
    grad_in = outer_sum(hidden_two, grad_upper)
    h2_part = times_transposed(grad_upper, my_in).astype(b16)
    down_sum, grad_h2 = scatter(
        3, (down_part.reshape(n_shard, tok_dev, width), h2_part.reshape(n_shard, tok_dev, width))
    )
    output = (resid + down_sum).astype(b16)
    norm_grad_two, grad_gain_two = norm_backward(grad_h2, normed_two, inverse_two, full_g2)
    grad_resid = own_grad.astype(f32) + norm_grad_two
    (resid_b,) = gather(4, (grad_resid.astype(b16),), (), (), n_shard)
    resid_b = resid_b.reshape(count, width)
    grad_out = outer_sum(attended, resid_b)
    grad_att = times_transposed(resid_b, out_weight).astype(b16)
    grad_heads = grad_att.reshape(count, heads, HEAD_DIM).transpose(1, 0, 2)
    delta = jnp.sum(grad_heads.astype(f32) * att_heads.astype(f32), axis=-1, keepdims=True)
    probs = expo / totals
    grad_value = jnp.einsum(
        "hqk,hqd->khd", probs.astype(b16), grad_heads, preferred_element_type=f32
    )
    grad_probs = jnp.einsum("hqd,hkd->hqk", grad_heads, values, preferred_element_type=f32)
    grad_scores = (probs * (grad_probs - delta) * scale).astype(b16)
    grad_qr = jnp.einsum("hqk,hkd->hqd", grad_scores, key_rot, preferred_element_type=f32)
    grad_kr = jnp.einsum("hqk,hqd->hkd", grad_scores, query_rot, preferred_element_type=f32)
    grad_q = (grad_qr * cosine - rotate_half(grad_qr) * sine).transpose(1, 0, 2)
    grad_k = (grad_kr * cosine - rotate_half(grad_kr) * sine).transpose(1, 0, 2)
    grad_projected = jnp.concatenate(
        [g.reshape(count, part) for g in (grad_q, grad_k, grad_value)], axis=-1
    ).astype(b16)
    grad_qkv = outer_sum(hidden_one, grad_projected)
    h1_part = times_transposed(grad_projected, my_qkv).astype(b16)
    def gain_rows(gain):
        room = -part % LANES
        rows = jnp.pad(gain.reshape(n_shard, part), ((0, 0), (0, room)))
        rows = rows.reshape(n_shard, -1, LANES)
        return jnp.pad(rows, ((0, 0), (0, 16 - rows.shape[1]), (0, 0))).astype(b16)

    sum_qkv, sum_g1, sum_in, sum_g2, sum_out, sum_down, grad_h1 = sum_over_rep(
        6,
        n_rep,
        grad_qkv.astype(b16).reshape(n_shard, part, -1),
        h1_part.reshape(n_shard, tok_dev, width),
        normed_one,
        grad_in.astype(b16).reshape(n_shard, part, -1),
        gain_rows(grad_gain_two),
        grad_out.astype(b16),
        grad_down.astype(b16),
    )
    norm_grad_one, _ = norm_backward(grad_h1, normed_one, inverse_one, full_g1)
    grad_tokens = grad_resid + norm_grad_one
    return (
        output.reshape(1, tok_dev, width),
        grad_tokens.reshape(1, tok_dev, width),
        sum_g1.reshape(-1)[:part],
        sum_qkv.astype(f32),
        sum_out.astype(f32),
        sum_g2.reshape(-1)[:part],
        sum_in.astype(f32),
        sum_down.astype(f32),
    )


def solution(mesh):
    in_specs = (
        P("rep", "shard", None),
        P("shard"),
        P("shard", None),
        P("shard", None),
        P("shard"),
        P("shard", None),
        P("shard", None),
        P("rep", "shard", None),
    )
    out_specs = (
        P("rep", "shard", None),
        P("rep", "shard", None),
        P("shard"),
        P("shard", None),
        P("shard", None),
        P("shard"),
        P("shard", None),
        P("shard", None),
    )
    body = functools.partial(local, mesh.shape["shard"], mesh.shape["rep"])
    return jax.shard_map(body, mesh=mesh, in_specs=in_specs, out_specs=out_specs, check_vma=False)
```
